128 devices in a mesh: band: 8 (over y, x_lo), loc: 16 (over z, x_hi, core).
Axes of the slice: x: 4 (x_hi: 2, x_lo: 2; x = x_hi * 2 + x_lo), y: 4, z: 4, core: 2. Of those that a mesh axis runs over, the one named last changes fastest.
Arguments:
- tokens: bfloat16 [4096, 16, 768], P('loc', 'band'), may hold values from -6 to 6
- band_index: int32 [16], replicated, may hold values from 0 to 15, each once
- band_table: float32 [16, 768], replicated, may hold values from -3 to 3
- window_ids: int32 [4096], replicated, may hold values from 0 to 1, as said below
- spatial_qkv: bfloat16 [768, 2304], replicated
- spatial_out: bfloat16 [768, 768], replicated, may hold values from -0.21875 to 0.21875
- channel_qkv: bfloat16 [768, 2304], replicated
- channel_out: bfloat16 [768, 768], replicated, may hold values from -0.21875 to 0.21875
- up_weight: bfloat16 [768, 3072], replicated, may hold values from -0.21875 to 0.21875
- down_weight: bfloat16 [3072, 768], replicated, may hold values from -0.109375 to 0.109375
Outputs:
- joined: bfloat16 [4096, 16, 768], P('loc', 'band')
The draws below stay inside these ranges and needn't reach their ends.
Inputs may be any that keep to these rules, and one draw needn't show every extreme that they name: `window_ids`: each of the 2 windows holds exactly 2048 locations, and each aligned block of 256 locations holds exactly 128 locations of each window. `band_index`: each of the 16 band numbers once.
All inputs are finite; a program needn't handle non-finite values.
Results may differ from the reference program's by a relative error of at most 0.014.
Values may be sent and summed in bfloat16 or wider, within the bound.
A program may use at most 128 MiB of HBM per device.

```python
import jax
import jax.numpy as jnp
from jax import lax

D = 768
HEADS = 12
HEAD_DIM = 64
FF = 3072
BANDS = 16
LOC_DEV = 256
WINDOWS = 2
LOCS = 4096


def draw_window_ids(key, part):
    blocks = LOCS // LOC_DEV
    keys = jax.random.split(jax.random.fold_in(key, 7), blocks)
    order = jax.vmap(lambda one: jax.random.permutation(one, LOC_DEV))(keys)
    return (order % WINDOWS).reshape(LOCS).astype(jnp.int32)


def projection_draw(key, salt):
    first, second, third = jax.random.split(jax.random.fold_in(key, salt), 3)
    factor = D ** (-0.5)
    w_query = jax.random.normal(first, (D, D), jnp.float32) * factor
    w_value = jax.random.normal(third, (D, D), jnp.float32) * factor
    w_key = jax.random.normal(second, (D, D), jnp.float32) * factor
    return jnp.concatenate([w_query, w_key, w_value], axis=1)


def draw_spatial_qkv(key, part):
    return projection_draw(key, 11).astype(jnp.bfloat16)


def draw_channel_qkv(key, part):
    return projection_draw(key, 23).astype(jnp.bfloat16)


def level_of(stream_key, shape, shards, smallest, top_value):
    factor_of = 1.0
    for position, blocks in shards:
        draws = jax.random.uniform(jax.random.fold_in(jax.random.fold_in(stream_key, 6), position), (blocks,), jnp.float32, smallest / len(shards), top_value / len(shards))
        factor_of = factor_of * jnp.repeat(jnp.exp(draws), shape[position] // blocks).reshape((-1,) + (1,) * (len(shape) - 1 - position))
    return factor_of


def noise(rng, extent, width, bound, pieces=(), kind=jnp.bfloat16):
    array = jax.random.normal(rng, extent, jnp.float32) * width
    if len(pieces) > 0:
        array = level_of(rng, extent, pieces, -0.22, 0.18) * array
    return jnp.clip(array, min=-bound, max=bound).astype(kind)


def setup_inputs(seed: int = 0) -> dict:
    splits = jax.random.split(jax.random.key(seed), 11)
    return {
        "tokens": noise(splits[0], (LOCS, BANDS, D), 1.0, 6.0, ((0, 16), (1, 8))),
        "band_index": jax.random.permutation(splits[1], BANDS).astype(jnp.int32),
        "band_table": noise(splits[2], (BANDS, D), 0.5, 3.0, (), jnp.float32),
        "window_ids": draw_window_ids(jax.random.fold_in(splits[10], 71), 0),
        "spatial_qkv": draw_spatial_qkv(jax.random.fold_in(splits[10], 71), 0),
        "spatial_out": noise(splits[5], (D, D), D ** -0.5, 0.21875),
        "channel_qkv": draw_channel_qkv(jax.random.fold_in(splits[10], 71), 0),
        "channel_out": noise(splits[7], (D, D), D ** -0.5, 0.21875),
        "up_weight": noise(splits[8], (D, FF), D ** -0.5, 0.21875),
        "down_weight": noise(splits[9], (FF, D), FF ** -0.5, 0.109375),
    }


def norm_rows(values):
    centre = values - lax.optimization_barrier(jnp.mean(values, axis=-1, keepdims=True))
    spread = lax.optimization_barrier(jnp.mean(centre * centre, axis=-1, keepdims=True))
    return centre * lax.rsqrt(spread + 1e-05)

def reference(tokens, band_index, band_table, window_ids, spatial_qkv, spatial_out, channel_qkv, channel_out, up_weight, down_weight):
    scale = HEAD_DIM ** (-0.5)
    onehot = (band_index[:, None] == jnp.arange(BANDS, dtype=jnp.int32)[None, :]).astype(jnp.float32)
    embed = jnp.dot(onehot, band_table, precision=lax.Precision.HIGHEST)
    start = tokens.astype(jnp.float32) + embed[None]
    normed = norm_rows(start).astype(jnp.bfloat16).reshape(-1, D)
    sqkv = jnp.dot(normed, spatial_qkv, preferred_element_type=jnp.float32).astype(jnp.bfloat16)
    sqkv = sqkv.reshape(LOCS, BANDS, 3, HEADS, HEAD_DIM)
    same = window_ids[:, None] == window_ids[None, :]

    def one_head(index):
        band = index // HEADS
        head = index % HEADS
        query = sqkv[:, band, 0, head]
        keys = sqkv[:, band, 1, head]
        values = sqkv[:, band, 2, head]
        scores = jnp.dot(query, keys.T, preferred_element_type=jnp.float32) * scale
        masked = jnp.where(same, scores, -1e+30)
        peak = lax.optimization_barrier(jnp.max(masked, axis=-1, keepdims=True))
        expo = jnp.where(same, jnp.exp(masked - peak), 0.0)
        total = lax.optimization_barrier(jnp.sum(expo, axis=-1, keepdims=True))
        summed = jnp.dot(expo.astype(jnp.bfloat16), values, preferred_element_type=jnp.float32)
        return (summed / total).astype(jnp.bfloat16)
    heads_out = lax.map(one_head, jnp.arange(BANDS * HEADS, dtype=jnp.int32))
    sattn = heads_out.reshape(BANDS, HEADS, LOCS, HEAD_DIM).transpose(2, 0, 1, 3).reshape(-1, D)
    mid = (start.reshape(-1, D) + jnp.dot(sattn, spatial_out, preferred_element_type=jnp.float32)).astype(jnp.bfloat16)
    normed2 = norm_rows(mid.astype(jnp.float32)).astype(jnp.bfloat16)
    cqkv = jnp.dot(normed2, channel_qkv, preferred_element_type=jnp.float32).astype(jnp.bfloat16)
    cqkv = cqkv.reshape(LOCS, BANDS, 3, HEADS, HEAD_DIM).astype(jnp.float32)
    cscores = jnp.einsum('lbhe,lche->lhbc', cqkv[:, :, 0], cqkv[:, :, 1]) * scale
    cpeak = lax.optimization_barrier(jnp.max(cscores, axis=-1, keepdims=True))
    cex = jnp.exp(cscores - cpeak)
    ctotal = lax.optimization_barrier(jnp.sum(cex, axis=-1))
    csum = jnp.einsum('lhbc,lche->lbhe', cex.astype(jnp.bfloat16).astype(jnp.float32), cqkv[:, :, 2])
    cattn = (csum / jnp.transpose(ctotal, (0, 2, 1))[..., None]).astype(jnp.bfloat16).reshape(-1, D)
    after = mid.astype(jnp.float32) + jnp.dot(cattn, channel_out, preferred_element_type=jnp.float32)
    normed3 = norm_rows(after).astype(jnp.bfloat16)
    hidden = jax.nn.gelu(jnp.dot(normed3, up_weight, preferred_element_type=jnp.float32), approximate=True).astype(jnp.bfloat16)
    joined = after + jnp.dot(hidden, down_weight, preferred_element_type=jnp.float32)
    return joined.astype(jnp.bfloat16).reshape(LOCS, BANDS, D)
```

```python
import functools

import jax
import jax.numpy as jnp
from jax import lax
from jax.experimental import pallas as pl
from jax.experimental.pallas import tpu as pltpu
from jax.sharding import PartitionSpec as P

BF = jnp.bfloat16
F32 = jnp.float32
MESH = pl.DeviceIdType.MESH
NT = (((1,), (1,)), ((), ()))
QSCALE = 0.125 * 1.4426950408889634


def norm_rows(values):
    centre = values - jnp.mean(values, axis=-1, keepdims=True)
    spread = jnp.mean(centre * centre, axis=-1, keepdims=True)
    return centre * lax.rsqrt(spread + 1e-05)


def place():
    band = lax.axis_index("band")
    loc = lax.axis_index("loc")
    return band // 2, band % 2, loc // 4, (loc // 2) % 2, loc % 2


def at(y, xlo, z, xhi, core):
    return {"band": y * 2 + xlo, "loc": z * 4 + xhi * 2 + core}


def spatial_kernel(
    tok_ref, tgt_ref, bi_ref, table_ref, w_hbm,
    sattn_ref, tokch_ref,
    perm, normed, xbuf, wbuf, qbuf, kbuf, vbuf, s0, s1, m0, m1, obuf,
    wsem, a_send, a_recv, f_send, c_send, c_recv, t_send, t_recv, t_local, o_send, o_recv,
):
    y, xlo, z, xhi, core = place()
    me = lax.axis_index("band")
    loc = lax.axis_index("loc")
    flip = z + 1 - 2 * (z % 2)
    opp = 3 - z

    first = 3 * (z % 2)
    wcopies = []
    for t in range(3):
        for n, pair in enumerate((first + core, first + 2)):
            cols = pl.ds(pl.multiple_of(t * 768 + pair * 128, 128), 128)
            wcopies.append(pltpu.make_async_copy(
                w_hbm.at[:, cols], wbuf.at[:, pl.ds(t * 256 + n * 128, 128)], wsem.at[2 * t + n]))
    for c in wcopies:
        c.start()

    rows = lax.broadcasted_iota(jnp.int32, (512, 512), 0)
    select = jnp.where(rows == tgt_ref[...], 1.0, 0.0).astype(BF)
    ordered = jnp.dot(select, tok_ref[...], preferred_element_type=F32)
    for b in range(2):
        part = ordered[b * 256:(b + 1) * 256]
        perm[b] = part.astype(BF).reshape(16, 16, 768)
        row = table_ref[pl.ds(bi_ref[2 * me + b], 1), :]
        nb = norm_rows(part + row).astype(BF)
        normed[2 * b] = nb[:128]
        normed[2 * b + 1] = nb[128:]

    sends = []
    slot = xhi * 4 + z
    mine = z // 2
    for b in range(2):
        for n, (w, zt) in enumerate(((mine, z), (mine, flip), (1 - mine, opp))):
            sends.append(pltpu.make_async_remote_copy(
                normed.at[2 * b + w], xbuf.at[slot], a_send.at[3 * b + n], a_recv.at[slot],
                device_id=at(y, 1 - xlo, zt, b, core), device_id_type=MESH))
    for s in (2, 0, 1, 5, 3, 4):
        sends[s].start()

    tsends = []
    for d in range(1, 8):
        to = (me + d) % 8
        for b in range(2):
            tsends.append(pltpu.make_async_remote_copy(
                perm.at[b, pl.ds(2 * to, 2)], tokch_ref.at[:, 2 * me + b],
                t_send.at[2 * d + b - 2], t_recv.at[2 * d + b - 2],
                device_id={"band": to, "loc": loc}, device_id_type=MESH))
    for c in tsends:
        c.start()
    tlocal = [pltpu.make_async_copy(
        perm.at[b, pl.ds(2 * me, 2)], tokch_ref.at[:, 2 * me + b], t_local.at[b]) for b in range(2)]
    for c in tlocal:
        c.start()

    for c in wcopies:
        c.wait()

    def project(s, shared_q):
        x = xbuf[s]
        q = jnp.dot(x, wbuf[:, 0:256], preferred_element_type=F32) * QSCALE
        qbuf[s] = q[:, :128].astype(BF)
        if shared_q:
            qbuf[16 + s] = q[:, 128:].astype(BF)
        k = jnp.dot(x, wbuf[:, 256:512], preferred_element_type=F32)
        kbuf[0, s] = k[:, :128].astype(BF)
        kbuf[1, s] = k[:, 128:].astype(BF)
        v = jnp.dot(x, wbuf[:, 512:768], preferred_element_type=F32)
        vt = v.T.astype(BF)
        for n in range(4):
            vbuf[n, s, 0:64, :] = vt[64 * n:64 * n + 64]

    ones = jnp.ones((16, 128), BF)

    def fill(s, _):
        for n in range(4):
            vbuf[n, s, 64:80, :] = ones
        return 0

    lax.fori_loop(0, 16, fill, 0)

    def arrival(s):
        return pltpu.make_async_remote_copy(
            xbuf.at[s], xbuf.at[s], c_send.at[s], a_recv.at[s],
            device_id=at(y, xlo, z, xhi, 1 - core), device_id_type=MESH)

    def to_partner(s):
        return pltpu.make_async_remote_copy(
            xbuf.at[s], xbuf.at[8 + s], c_send.at[s], c_recv.at[s],
            device_id=at(y, xlo, z, xhi, 1 - core), device_id_type=MESH)

    def forward(s, n):
        return pltpu.make_async_remote_copy(
            xbuf.at[s], xbuf.at[s], f_send.at[n], a_recv.at[s],
            device_id=at(y, xlo, flip, xhi, core), device_id_type=MESH)

    for n in range(2):
        s = n * 4 + opp
        arrival(s).wait_recv()
        forward(s, n).start()
        to_partner(s).start()

    for zs in (z, flip, 3 - flip):
        for n in range(2):
            s = n * 4 + zs
            arrival(s).wait_recv()
            to_partner(s).start()

    def project_own(s, _):
        project(s, True)
        return 0

    lax.fori_loop(0, 8, project_own, 0)

    def project_other(s, _):
        to_partner(s).wait_recv()
        project(8 + s, False)
        return 0

    lax.fori_loop(0, 8, project_other, 0)

    lane = lax.broadcasted_iota(jnp.int32, (256, 128), 1)

    def scores(u, h, sref, mref):
        kv = u // 8
        q = qbuf[pl.ds(2 * u, 2)].reshape(256, 128)
        q = jnp.where((lane < 64) == (h == 0), q, jnp.zeros_like(q))
        peak = None
        for c in range(8):
            keys = kbuf[kv, pl.ds(2 * c, 2)].reshape(256, 128)
            st = lax.dot_general(keys, q, NT, preferred_element_type=F32)
            sref[pl.ds(c * 256, 256), :] = st
            top = jnp.max(st.reshape(32, 8, 256), axis=0)
            peak = top if peak is None else jnp.maximum(peak, top)
        mref[...] = jnp.broadcast_to(jnp.max(peak, axis=0, keepdims=True), (8, 256))

    def mix(u, h, sref, mref):
        kv = u // 8
        peak = mref[0:1, :]
        acc = None
        for c in range(8):
            p = jnp.exp2(sref[pl.ds(c * 256, 256), :] - peak).astype(BF)
            for n in range(2):
                part = jnp.dot(vbuf[kv * 2 + h, 2 * c + n], p[128 * n:128 * n + 128],
                               preferred_element_type=F32)
                acc = part if acc is None else acc + part
        return acc[:64] / acc[64:65]

    w = z // 2
    band = 2 * (y * 2 + 1 - xlo) + xhi

    def message(i, jj):
        s = i % 16
        src_core = (core + s // 8) % 2
        xs = (s % 8) // 4
        zs = s % 4
        pair = first + jnp.where(i < 16, core, 2)
        to_band = w * 4 + jj
        to_loc = zs * 4 + xs * 2 + src_core
        src = obuf.at[pl.ds(8 * i + 2 * jj, 2)]
        dst = sattn_ref.at[:, band, :, pl.ds(pl.multiple_of(pair * 128, 128), 128)]
        is_self = jnp.logical_and(to_band == me, to_loc == loc)
        remote = pltpu.make_async_remote_copy(
            src, dst, o_send, o_recv, device_id={"band": to_band, "loc": to_loc},
            device_id_type=MESH)
        return is_self, remote, pltpu.make_async_copy(src, dst, o_recv)

    def send_out(i):
        def one(jj, _):
            is_self, remote, local = message(i, jj)

            @pl.when(is_self)
            def _():
                local.start()

            @pl.when(jnp.logical_not(is_self))
            def _():
                remote.start()

            return 0

        lax.fori_loop(0, 4, one, 0)

    scores(0, 0, s0, m0)

    def unit(u, _):
        @pl.when(u > 0)
        def _():
            send_out(2 * u - 2)
            send_out(2 * u - 1)

        scores(u, 1, s1, m1)
        a = mix(u, 0, s0, m0)
        scores(jnp.minimum(u + 1, 11), 0, s0, m0)
        b = mix(u, 1, s1, m1)
        o = jnp.concatenate([a, b], axis=0).T.astype(BF)
        obuf[pl.ds(16 * u, 16)] = o.reshape(16, 16, 128)
        return 0

    lax.fori_loop(0, 12, unit, 0)
    send_out(22)
    send_out(23)

    for c in sends:
        c.wait_send()
    for n in range(2):
        forward(n * 4 + opp, n).wait_send()

    def core_done(s, _):
        to_partner(s).wait_send()
        return 0

    lax.fori_loop(0, 8, core_done, 0)
    for c in tsends:
        c.wait_send()
        c.wait_recv()
    for c in tlocal:
        c.wait()

    stays = me // 4 == w

    @pl.when(stays)
    def _():
        pltpu.make_async_copy(obuf.at[pl.ds(0, 188)], obuf.at[pl.ds(0, 188)], o_send).wait()

    @pl.when(jnp.logical_not(stays))
    def _():
        pltpu.make_async_copy(obuf, obuf, o_send).wait()

    pltpu.make_async_copy(sattn_ref, sattn_ref, o_recv).wait()


def spatial(tokens, tgt, band_index, table, spatial_qkv):
    vmem = pl.BlockSpec(memory_space=pltpu.VMEM)
    hbm = pl.BlockSpec(memory_space=pl.ANY)
    dma = pltpu.SemaphoreType.DMA
    return pl.pallas_call(
        spatial_kernel,
        out_shape=[jax.ShapeDtypeStruct((2, 16, 16, 768), BF)] * 2,
        in_specs=[vmem, vmem, pl.BlockSpec(memory_space=pltpu.SMEM), vmem, hbm],
        out_specs=[hbm, hbm],
        scratch_shapes=[
            pltpu.VMEM((2, 16, 16, 768), BF),
            pltpu.VMEM((4, 128, 768), BF),
            pltpu.VMEM((16, 128, 768), BF),
            pltpu.VMEM((768, 768), BF),
            pltpu.VMEM((24, 128, 128), BF),
            pltpu.VMEM((2, 16, 128, 128), BF),
            pltpu.VMEM((4, 16, 80, 128), BF),
            pltpu.VMEM((2048, 256), F32),
            pltpu.VMEM((2048, 256), F32),
            pltpu.VMEM((8, 256), F32),
            pltpu.VMEM((8, 256), F32),
            pltpu.VMEM((192, 16, 128), BF),
            dma((6,)), dma((6,)), dma((8,)), dma((2,)), dma((8,)), dma((8,)),
            dma((14,)), dma((14,)), dma((2,)), dma, dma,
        ],
        compiler_params=pltpu.CompilerParams(
            has_side_effects=True, vmem_limit_bytes=60 << 20),
        name="spatial",
    )(tokens, tgt, band_index, table, spatial_qkv)


def channel_kernel(
    sattn_ref, tokch_ref, bi_ref, table_ref, tgt_ref, wo_h, wc_h, wco_h, wu_h, wd_h,
    out_ref,
    wo, wc, wco, wu, wd, sa, tk, jbuf, outp,
    cat, hid, wsem, isem, j_send, j_recv, j_local,
):
    me = lax.axis_index("band")
    loc = lax.axis_index("loc")
    icopies = [pltpu.make_async_copy(sattn_ref, sa, isem.at[0]),
               pltpu.make_async_copy(tokch_ref, tk, isem.at[1])]
    for c in icopies:
        c.start()
    wcopies = [pltpu.make_async_copy(src, dst, wsem.at[n]) for n, (src, dst) in enumerate(
        ((wo_h, wo), (wc_h, wc), (wco_h, wco), (wu_h, wu), (wd_h, wd)))]
    for c in wcopies:
        c.start()
    barrier = pltpu.get_barrier_semaphore()
    for d in range(1, 8):
        pl.semaphore_signal(barrier, inc=1, device_id={"band": (me + d) % 8, "loc": loc},
                            device_id_type=MESH)
    pl.semaphore_wait(barrier, 7)
    for c in icopies:
        c.wait()
    for c in wcopies:
        c.wait()

    embed = jnp.concatenate([table_ref[pl.ds(bi_ref[n], 1), :] for n in range(16)], axis=0)
    rowi = lax.broadcasted_iota(jnp.int32, (256, 256), 0)
    coli = lax.broadcasted_iota(jnp.int32, (256, 256), 1)
    same = (rowi % 16) == (coli % 16)
    lane = lax.broadcasted_iota(jnp.int32, (256, 128), 1)

    def message(h, d):
        to = (me + d) % 8
        return pltpu.make_async_remote_copy(
            jbuf.at[h, pl.ds(2 * to, 2)], outp.at[:, 2 * me + h],
            j_send.at[8 * h + d], j_recv.at[8 * h + d],
            device_id={"band": to, "loc": loc}, device_id_type=MESH)

    def local(h):
        return pltpu.make_async_copy(
            jbuf.at[h, pl.ds(2 * me, 2)], outp.at[:, 2 * me + h], j_local.at[h])

    def half(h, _):
        start = (tk[h].astype(F32) + embed[:, None, :]).reshape(256, 768)
        mid = (start + jnp.dot(sa[h].reshape(256, 768), wo[...],
                               preferred_element_type=F32)).astype(BF)
        midf = mid.astype(F32)
        normed = norm_rows(midf).astype(BF)
        for pair in range(6):
            cols = pl.ds(pair * 128, 128)
            q = (jnp.dot(normed, wc[:, cols], preferred_element_type=F32) * QSCALE).astype(BF)
            k = jnp.dot(normed, wc[:, pl.ds(768 + pair * 128, 128)],
                        preferred_element_type=F32).astype(BF)
            v = jnp.dot(normed, wc[:, pl.ds(1536 + pair * 128, 128)],
                        preferred_element_type=F32).astype(BF)
            vx = jnp.concatenate([v, jnp.ones((256, 128), BF)], axis=1)
            res = []
            for n in range(2):
                qn = jnp.where((lane < 64) == (n == 0), q, jnp.zeros_like(q))
                s = lax.dot_general(qn, k, NT, preferred_element_type=F32)
                s = jnp.where(same, s, -1e30)
                p = jnp.exp2(s - jnp.max(s, axis=1, keepdims=True)).astype(BF)
                r = jnp.dot(p, vx, preferred_element_type=F32)
                res.append(r[:, :128] / r[:, 128:])
            cat[:, cols] = jnp.where(lane < 64, res[0], res[1]).astype(BF)
        after = midf + jnp.dot(cat[...], wco[...], preferred_element_type=F32)
        normed = norm_rows(after).astype(BF)
        for c in range(4):
            cols = pl.ds(c * 768, 768)
            up = jnp.dot(normed, wu[:, cols], preferred_element_type=F32)
            hid[:, cols] = jax.nn.gelu(up, approximate=True).astype(BF)
        joined = after + jnp.dot(hid[...], wd[...], preferred_element_type=F32)
        jbuf[h] = joined.astype(BF).reshape(16, 16, 768)
        for d in range(1, 8):
            message(h, d).start()
        local(h).start()
        return 0

    lax.fori_loop(0, 2, half, 0)
    for h in range(2):
        local(h).wait()
        for d in range(1, 8):
            message(h, d).wait_send()
            message(h, d).wait_recv()
    cols = lax.broadcasted_iota(jnp.int32, (512, 512), 1)
    select = jnp.where(cols == tgt_ref[...], 1.0, 0.0).astype(BF)
    out_ref[...] = jnp.dot(select, outp[...].reshape(512, 768),
                           preferred_element_type=F32).astype(BF)


def channel(sattn, tokch, band_index, table, tgt, weights):
    vmem = pl.BlockSpec(memory_space=pltpu.VMEM)
    hbm = pl.BlockSpec(memory_space=pl.ANY)
    dma = pltpu.SemaphoreType.DMA
    return pl.pallas_call(
        channel_kernel,
        out_shape=jax.ShapeDtypeStruct((512, 768), BF),
        in_specs=[hbm, hbm, pl.BlockSpec(memory_space=pltpu.SMEM), vmem, vmem] + [hbm] * 5,
        out_specs=vmem,
        scratch_shapes=[pltpu.VMEM(w.shape, BF) for w in weights] + [
            pltpu.VMEM((2, 16, 16, 768), BF),
            pltpu.VMEM((2, 16, 16, 768), BF),
            pltpu.VMEM((2, 16, 16, 768), BF),
            pltpu.VMEM((2, 16, 16, 768), BF),
            pltpu.VMEM((256, 768), BF),
            pltpu.VMEM((256, 3072), BF),
            dma((5,)), dma((2,)), dma((16,)), dma((16,)), dma((2,)),
        ],
        compiler_params=pltpu.CompilerParams(
            has_side_effects=True, vmem_limit_bytes=60 << 20, collective_id=1),
        name="channel",
    )(sattn, tokch, band_index, table, tgt, *weights)


def body(
    tokens, band_index, band_table, window_ids, spatial_qkv, spatial_out,
    channel_qkv, channel_out, up_weight, down_weight,
):
    loc_dev = tokens.shape[0]
    ids = lax.dynamic_slice_in_dim(window_ids, lax.axis_index("loc") * loc_dev, loc_dev)
    earlier = jnp.arange(loc_dev)[None, :] < jnp.arange(loc_dev)[:, None]
    rank = jnp.sum(jnp.where((ids[:, None] == ids[None, :]) & earlier, 1, 0), axis=1)
    pos = (ids * 128 + rank).astype(jnp.int32)
    tgt = pos[:, None] + jnp.array([[0, 256]], jnp.int32)
    sattn, tokch = spatial(
        tokens.reshape(512, 768), tgt.reshape(1, 512), band_index, band_table, spatial_qkv)
    out = channel(
        sattn, tokch, band_index, band_table, tgt.reshape(512, 1),
        (spatial_out, channel_qkv, channel_out, up_weight, down_weight))
    return out.reshape(tokens.shape)


def solution(mesh):
    placed = (P("loc", "band", None), P(), P(), P(), P(), P(), P(), P(), P(), P())
    return jax.shard_map(
        body, mesh=mesh, in_specs=placed, out_specs=P("loc", "band", None), check_vma=False
    )
```

```python
import functools

import jax
import jax.numpy as jnp
from jax import lax
from jax.experimental import pallas as pl
from jax.experimental.pallas import tpu as pltpu
from jax.sharding import PartitionSpec as P

BF = jnp.bfloat16
F32 = jnp.float32
MESH = pl.DeviceIdType.MESH
NT = (((1,), (1,)), ((), ()))
QSCALE = 0.125 * 1.4426950408889634


def norm_rows(values):
    centre = values - jnp.mean(values, axis=-1, keepdims=True)
    spread = jnp.mean(centre * centre, axis=-1, keepdims=True)
    return centre * lax.rsqrt(spread + 1e-05)


def place():
    band = lax.axis_index("band")
    loc = lax.axis_index("loc")
    return band // 2, band % 2, loc // 4, (loc // 2) % 2, loc % 2


def at(y, xlo, z, xhi, core):
    return {"band": y * 2 + xlo, "loc": z * 4 + xhi * 2 + core}


def layer_kernel(
    tok_ref, tgtr_ref, tgtc_ref, bi_ref, table_ref, w_hbm, wo_h, wc_h, wco_h, wu_h, wd_h,
    out_ref,
    perm, normed, xbuf, wbuf, qbuf, kbuf, vbuf, s0, s1, m0, m1, obuf,
    wo, wc, wco, wu, wd, sattn_ref, tokch_ref, jbuf, outp, cat, qc, kc, vc, hid,
    wsem, a_send, a_recv, f_send, c_send, c_recv, t_send, t_recv, t_local, o_send, o_recv,
    lsem, j_send, j_recv, j_local,
):
    y, xlo, z, xhi, core = place()
    me = lax.axis_index("band")
    loc = lax.axis_index("loc")
    flip = z + 1 - 2 * (z % 2)
    opp = 3 - z

    first = 3 * (z % 2)
    wcopies = []
    for t in range(3):
        for n, pair in enumerate((first + core, first + 2)):
            cols = pl.ds(pl.multiple_of(t * 768 + pair * 128, 128), 128)
            wcopies.append(pltpu.make_async_copy(
                w_hbm.at[:, cols], wbuf.at[:, pl.ds(t * 256 + n * 128, 128)], wsem.at[2 * t + n]))
    for c in wcopies:
        c.start()
    lcopies = [pltpu.make_async_copy(src, dst, lsem.at[n]) for n, (src, dst) in enumerate(
        ((wo_h, wo), (wc_h, wc), (wco_h, wco), (wu_h, wu), (wd_h, wd)))]
    for c in lcopies:
        c.start()

    rows = lax.broadcasted_iota(jnp.int32, (512, 512), 0)
    select = jnp.where(rows == tgtr_ref[...], 1.0, 0.0).astype(BF)
    ordered = jnp.dot(select, tok_ref[...], preferred_element_type=F32)
    for b in range(2):
        part = ordered[b * 256:(b + 1) * 256]
        perm[b] = part.astype(BF).reshape(16, 16, 768)
        row = table_ref[pl.ds(bi_ref[2 * me + b], 1), :]
        nb = norm_rows(part + row).astype(BF)
        normed[2 * b] = nb[:128]
        normed[2 * b + 1] = nb[128:]

    sends = []
    slot = xhi * 4 + z
    mine = z // 2
    for b in range(2):
        for n, (w, zt) in enumerate(((mine, z), (mine, flip), (1 - mine, opp))):
            sends.append(pltpu.make_async_remote_copy(
                normed.at[2 * b + w], xbuf.at[slot], a_send.at[3 * b + n], a_recv.at[slot],
                device_id=at(y, 1 - xlo, zt, b, core), device_id_type=MESH))
    for s in (1, 4, 2, 5, 0, 3):
        sends[s].start()

    tsends = []
    for d in range(1, 8):
        to = (me + d) % 8
        for b in range(2):
            tsends.append(pltpu.make_async_remote_copy(
                perm.at[b, pl.ds(2 * to, 2)], tokch_ref.at[:, 2 * me + b],
                t_send.at[2 * d + b - 2], t_recv.at[2 * d + b - 2],
                device_id={"band": to, "loc": loc}, device_id_type=MESH))
    for c in tsends:
        c.start()
    tlocal = [pltpu.make_async_copy(
        perm.at[b, pl.ds(2 * me, 2)], tokch_ref.at[:, 2 * me + b], t_local.at[b]) for b in range(2)]
    for c in tlocal:
        c.start()

    for c in wcopies:
        c.wait()

    def project(s, shared_q):
        x = xbuf[s]
        q = jnp.dot(x, wbuf[:, 0:256], preferred_element_type=F32) * QSCALE
        qbuf[s] = q[:, :128].astype(BF)
        if shared_q:
            qbuf[16 + s] = q[:, 128:].astype(BF)
        k = jnp.dot(x, wbuf[:, 256:512], preferred_element_type=F32)
        kbuf[0, s] = k[:, :128].astype(BF)
        kbuf[1, s] = k[:, 128:].astype(BF)
        v = jnp.dot(x, wbuf[:, 512:768], preferred_element_type=F32)
        vt = v.T.astype(BF)
        for n in range(4):
            vbuf[n, s, 0:64, :] = vt[64 * n:64 * n + 64]

    ones = jnp.ones((16, 128), BF)

    def fill(s, _):
        for n in range(4):
            vbuf[n, s, 64:80, :] = ones
        return 0

    lax.fori_loop(0, 16, fill, 0)

    def arrival(s):
        return pltpu.make_async_remote_copy(
            xbuf.at[s], xbuf.at[s], c_send.at[s], a_recv.at[s],
            device_id=at(y, xlo, z, xhi, 1 - core), device_id_type=MESH)

    def to_partner(s):
        return pltpu.make_async_remote_copy(
            xbuf.at[s], xbuf.at[8 + s], c_send.at[s], c_recv.at[s],
            device_id=at(y, xlo, z, xhi, 1 - core), device_id_type=MESH)

    def forward(s, n):
        return pltpu.make_async_remote_copy(
            xbuf.at[s], xbuf.at[s], f_send.at[n], a_recv.at[s],
            device_id=at(y, xlo, flip, xhi, core), device_id_type=MESH)

    def source(t):
        r = t // 2
        zs = jnp.where(r == 0, flip, jnp.where(r == 1, opp, jnp.where(r == 2, z, 3 - flip)))
        return (t % 2) * 4 + zs

    def arrive(t, _):
        @pl.when(t < 8)
        def _():
            s = source(t)
            arrival(s).wait_recv()
            to_partner(s).start()

            @pl.when(t // 2 == 1)
            def _():
                forward(s, t % 2).start()

            project(s, True)

        @pl.when(t >= 2)
        def _():
            s = source(t - 2)
            to_partner(s).wait_recv()
            project(8 + s, False)

        return 0

    lax.fori_loop(0, 10, arrive, 0)

    lane = lax.broadcasted_iota(jnp.int32, (256, 128), 1)

    def scores(u, h, sref, mref):
        kv = u // 8
        q = qbuf[pl.ds(2 * u, 2)].reshape(256, 128)
        q = jnp.where((lane < 64) == (h == 0), q, jnp.zeros_like(q))
        peak = None
        for c in range(8):
            keys = kbuf[kv, pl.ds(2 * c, 2)].reshape(256, 128)
            st = lax.dot_general(keys, q, NT, preferred_element_type=F32)
            sref[pl.ds(c * 256, 256), :] = st
            top = jnp.max(st.reshape(32, 8, 256), axis=0)
            peak = top if peak is None else jnp.maximum(peak, top)
        mref[...] = jnp.broadcast_to(jnp.max(peak, axis=0, keepdims=True), (8, 256))

    def mix(u, h, sref, mref):
        kv = u // 8
        peak = mref[0:1, :]
        acc = None
        for c in range(8):
            p = jnp.exp2(sref[pl.ds(c * 256, 256), :] - peak).astype(BF)
            for n in range(2):
                part = jnp.dot(vbuf[kv * 2 + h, 2 * c + n], p[128 * n:128 * n + 128],
                               preferred_element_type=F32)
                acc = part if acc is None else acc + part
        return acc[:64] / acc[64:65]

    w = z // 2
    band = 2 * (y * 2 + 1 - xlo) + xhi

    def send_out(i):
        s = i % 16
        src_core = (core + s // 8) % 2
        xs = (s % 8) // 4
        zs = s % 4
        pair = first + jnp.where(i < 16, core, 2)
        to_loc = zs * 4 + xs * 2 + src_core
        cols = pl.ds(pl.multiple_of(pair * 128, 128), 128)
        dst = sattn_ref.at[:, band, :, cols]

        def remote(jj):
            pltpu.make_async_remote_copy(
                obuf.at[pl.ds(8 * i + 2 * jj, 2)], dst, o_send, o_recv,
                device_id={"band": w * 4 + jj, "loc": to_loc}, device_id_type=MESH).start()

        own = jnp.logical_and(me // 4 == w, to_loc == loc)

        @pl.when(own)
        def _():
            for jj in range(4):
                @pl.when(w * 4 + jj == me)
                def _():
                    pltpu.make_async_copy(
                        obuf.at[pl.ds(8 * i + 2 * jj, 2)], dst, o_recv).start()

                @pl.when(w * 4 + jj != me)
                def _():
                    remote(jj)

        @pl.when(jnp.logical_not(own))
        def _():
            for jj in range(4):
                remote(jj)

    scores(0, 0, s0, m0)

    def unit(u, _):
        @pl.when(u > 0)
        def _():
            send_out(2 * u - 2)
            send_out(2 * u - 1)

        scores(u, 1, s1, m1)
        a = mix(u, 0, s0, m0)
        scores(jnp.minimum(u + 1, 11), 0, s0, m0)
        b = mix(u, 1, s1, m1)
        o = jnp.concatenate([a, b], axis=0).T.astype(BF)
        obuf[pl.ds(16 * u, 16)] = o.reshape(16, 16, 128)
        return 0

    lax.fori_loop(0, 12, unit, 0)
    send_out(22)
    send_out(23)

    for c in sends:
        c.wait_send()
    for n in range(2):
        forward(n * 4 + opp, n).wait_send()

    def core_done(s, _):
        to_partner(s).wait_send()
        return 0

    lax.fori_loop(0, 8, core_done, 0)
    for c in tsends:
        c.wait_send()
        c.wait_recv()
    for c in tlocal:
        c.wait()

    stays = me // 4 == w

    @pl.when(stays)
    def _():
        pltpu.make_async_copy(obuf.at[pl.ds(0, 188)], obuf.at[pl.ds(0, 188)], o_send).wait()

    @pl.when(jnp.logical_not(stays))
    def _():
        pltpu.make_async_copy(obuf, obuf, o_send).wait()

    pltpu.make_async_copy(sattn_ref, sattn_ref, o_recv).wait()

    embed = jnp.concatenate([table_ref[pl.ds(bi_ref[n], 1), :] for n in range(16)], axis=0)
    rowi = lax.broadcasted_iota(jnp.int32, (256, 256), 0)
    coli = lax.broadcasted_iota(jnp.int32, (256, 256), 1)
    same = (rowi % 16) == (coli % 16)

    def home(h, d):
        to = (me + d) % 8
        return pltpu.make_async_remote_copy(
            jbuf.at[h, pl.ds(2 * to, 2)], outp.at[:, 2 * me + h],
            j_send.at[8 * h + d], j_recv.at[8 * h + d],
            device_id={"band": to, "loc": loc}, device_id_type=MESH)

    def local(h):
        return pltpu.make_async_copy(
            jbuf.at[h, pl.ds(2 * me, 2)], outp.at[:, 2 * me + h], j_local.at[h])

    def half(h, _):
        start = (tokch_ref[h].astype(F32) + embed[:, None, :]).reshape(256, 768)
        mid = (start + jnp.dot(sattn_ref[h].reshape(256, 768), wo[...],
                               preferred_element_type=F32)).astype(BF)
        midf = mid.astype(F32)
        normed = norm_rows(midf).astype(BF)
        qc[...] = (jnp.dot(normed, wc[:, 0:768], preferred_element_type=F32) * QSCALE).astype(BF)
        kc[...] = jnp.dot(normed, wc[:, 768:1536], preferred_element_type=F32).astype(BF)
        vc[...] = jnp.dot(normed, wc[:, 1536:2304], preferred_element_type=F32).astype(BF)
        for pair in range(6):
            cols = pl.ds(pair * 128, 128)
            q = qc[:, cols]
            k = kc[:, cols]
            vx = jnp.concatenate([vc[:, cols], jnp.ones((256, 128), BF)], axis=1)
            res = []
            for n in range(2):
                qn = jnp.where((lane < 64) == (n == 0), q, jnp.zeros_like(q))
                s = lax.dot_general(qn, k, NT, preferred_element_type=F32)
                s = jnp.where(same, s, -1e30)
                p = jnp.exp2(s - jnp.max(s, axis=1, keepdims=True)).astype(BF)
                r = jnp.dot(p, vx, preferred_element_type=F32)
                res.append(r[:, :128] / r[:, 128:])
            cat[:, cols] = jnp.where(lane < 64, res[0], res[1]).astype(BF)
        after = midf + jnp.dot(cat[...], wco[...], preferred_element_type=F32)
        normed = norm_rows(after).astype(BF)
        for c in range(4):
            cols = pl.ds(c * 768, 768)
            up = jnp.dot(normed, wu[:, cols], preferred_element_type=F32)
            hid[:, cols] = jax.nn.gelu(up, approximate=True).astype(BF)
        joined = after + jnp.dot(hid[...], wd[...], preferred_element_type=F32)
        jbuf[h] = joined.astype(BF).reshape(16, 16, 768)
        for d in range(1, 8):
            home(h, d).start()
        local(h).start()
        return 0

    for c in lcopies:
        c.wait()
    lax.fori_loop(0, 2, half, 0)
    for h in range(2):
        local(h).wait()
        for d in range(1, 8):
            home(h, d).wait_send()
            home(h, d).wait_recv()
    cols = lax.broadcasted_iota(jnp.int32, (512, 512), 1)
    select = jnp.where(cols == tgtc_ref[...], 1.0, 0.0).astype(BF)
    out_ref[...] = jnp.dot(select, outp[...].reshape(512, 768),
                           preferred_element_type=F32).astype(BF)


def layer(tokens, tgt_row, tgt_col, band_index, table, spatial_qkv, weights):
    vmem = pl.BlockSpec(memory_space=pltpu.VMEM)
    hbm = pl.BlockSpec(memory_space=pl.ANY)
    dma = pltpu.SemaphoreType.DMA
    rows = pltpu.VMEM((2, 16, 16, 768), BF)
    return pl.pallas_call(
        layer_kernel,
        out_shape=jax.ShapeDtypeStruct((512, 768), BF),
        in_specs=[vmem, vmem, vmem, pl.BlockSpec(memory_space=pltpu.SMEM), vmem] + [hbm] * 6,
        out_specs=vmem,
        scratch_shapes=[
            rows,
            pltpu.VMEM((4, 128, 768), BF),
            pltpu.VMEM((16, 128, 768), BF),
            pltpu.VMEM((768, 768), BF),
            pltpu.VMEM((24, 128, 128), BF),
            pltpu.VMEM((2, 16, 128, 128), BF),
            pltpu.VMEM((4, 16, 80, 128), BF),
            pltpu.VMEM((2048, 256), F32),
            pltpu.VMEM((2048, 256), F32),
            pltpu.VMEM((8, 256), F32),
            pltpu.VMEM((8, 256), F32),
            pltpu.VMEM((192, 16, 128), BF),
        ] + [pltpu.VMEM(w.shape, BF) for w in weights] + [
            rows, rows, rows, rows,
            pltpu.VMEM((256, 768), BF),
            pltpu.VMEM((256, 768), BF),
            pltpu.VMEM((256, 768), BF),
            pltpu.VMEM((256, 768), BF),
            pltpu.VMEM((256, 3072), BF),
            dma((6,)), dma((6,)), dma((8,)), dma((2,)), dma((8,)), dma((8,)),
            dma((14,)), dma((14,)), dma((2,)), dma, dma,
            dma((5,)), dma((16,)), dma((16,)), dma((2,)),
        ],
        compiler_params=pltpu.CompilerParams(
            has_side_effects=True, vmem_limit_bytes=60 << 20),
        name="layer",
    )(tokens, tgt_row, tgt_col, band_index, table, spatial_qkv, *weights)


def body(
    tokens, band_index, band_table, window_ids, spatial_qkv, spatial_out,
    channel_qkv, channel_out, up_weight, down_weight,
):
    loc_dev = tokens.shape[0]
    ids = lax.dynamic_slice_in_dim(window_ids, lax.axis_index("loc") * loc_dev, loc_dev)
    earlier = jnp.arange(loc_dev)[None, :] < jnp.arange(loc_dev)[:, None]
    rank = jnp.sum(jnp.where((ids[:, None] == ids[None, :]) & earlier, 1, 0), axis=1)
    pos = (ids * 128 + rank).astype(jnp.int32)
    tgt = pos[:, None] + jnp.array([[0, 256]], jnp.int32)
    out = layer(
        tokens.reshape(512, 768), tgt.reshape(1, 512), tgt.reshape(512, 1), band_index, band_table,
        spatial_qkv, (spatial_out, channel_qkv, channel_out, up_weight, down_weight))
    return out.reshape(tokens.shape)


def solution(mesh):
    placed = (P("loc", "band", None), P(), P(), P(), P(), P(), P(), P(), P(), P())
    return jax.shard_map(
        body, mesh=mesh, in_specs=placed, out_specs=P("loc", "band", None), check_vma=False
    )
```

```python
import functools

import jax
import jax.numpy as jnp
from jax import lax
from jax.experimental import pallas as pl
from jax.experimental.pallas import tpu as pltpu
from jax.sharding import PartitionSpec as P

BF = jnp.bfloat16
F32 = jnp.float32
MESH = pl.DeviceIdType.MESH
NT = (((1,), (1,)), ((), ()))
TOK = 6
QSCALE = 0.125 * 1.4426950408889634


def norm_rows(values):
    centre = values - jnp.mean(values, axis=-1, keepdims=True)
    spread = jnp.mean(centre * centre, axis=-1, keepdims=True)
    return centre * lax.rsqrt(spread + 1e-05)


def place():
    band = lax.axis_index("band")
    loc = lax.axis_index("loc")
    return band // 2, band % 2, loc // 4, (loc // 2) % 2, loc % 2


def at(y, xlo, z, xhi, core):
    return {"band": y * 2 + xlo, "loc": z * 4 + xhi * 2 + core}


def layer_kernel(
    tok_ref, ids_ref, bi_ref, table_ref, w_hbm, wo_h, wc_h, wco_h, wu_h, wd_h,
    out_ref,
    perm, normed, xbuf, wbuf, qbuf, kbuf, vbuf, s0, s1, m0, m1, obuf,
    choose, rbuf, wo, wc, wco, wu, wd, sattn_ref, tokch_ref, jbuf, outp, cat, nrm, aft, qc, kc, vc, hid,
    wsem, a_send, a_recv, f_send, c_send, c_recv, r_send, r_recv, rf_send, t_send, t_recv, t_local, o_send, o_recv,
    lsem, j_send, j_recv, j_local,
):
    y, xlo, z, xhi, core = place()
    me = lax.axis_index("band")
    loc = lax.axis_index("loc")

    def pairing(odd):
        turned = (z + 3 * odd) % 4
        beside = turned + 1 - 2 * (turned % 2)
        return turned, (beside + odd) % 4, (3 - turned + odd) % 4, (3 - beside + odd) % 4

    turned, flip, opp, far = pairing(xlo)
    sturned, sflip, sopp, _ = pairing(1 - xlo)
    w = turned // 2
    sw = sturned // 2

    first = 3 * (turned % 2)
    wcopies = []
    for t in range(3):
        for n, pair in enumerate((first + core, first + 2)):
            cols = pl.ds(pl.multiple_of(t * 768 + pair * 128, 128), 128)
            wcopies.append(pltpu.make_async_copy(
                w_hbm.at[:, cols], wbuf.at[:, pl.ds(t * 256 + n * 128, 128)], wsem.at[2 * t + n]))
    for c in wcopies:
        c.start()
    lcopies = [pltpu.make_async_copy(src, dst, lsem.at[n]) for n, (src, dst) in enumerate(
        ((wo_h, wo), (wc_h, wc), (wco_h, wco), (wu_h, wu), (wd_h, wd)))]
    for c in lcopies:
        c.start()

    ids = jnp.concatenate(
        [ids_ref[pl.ds(2 * loc, 1), :], ids_ref[pl.ds(2 * loc + 1, 1), :]], axis=1)
    down = lax.broadcasted_iota(jnp.int32, (256, 256), 0)
    across = lax.broadcasted_iota(jnp.int32, (256, 256), 1)
    ones_row = jnp.broadcast_to(ids.astype(F32), (8, 256)).astype(BF)
    earlier = jnp.where(down < across, 1.0, 0.0).astype(BF)
    before = jnp.dot(ones_row, earlier, preferred_element_type=F32)[0:1].astype(jnp.int32)
    count = lax.broadcasted_iota(jnp.int32, (1, 256), 1) - before
    target = jnp.where(ids == 1, 128 + before, count)
    select = jnp.where(down == target, 1.0, 0.0).astype(BF)
    choose[...] = select
    for b in range(2):
        part = jnp.dot(select, tok_ref[:, b, :], preferred_element_type=F32)
        perm[b] = part.astype(BF).reshape(16, 16, 768)
        row = table_ref[pl.ds(bi_ref[2 * me + b], 1), :]
        nb = norm_rows(part + row).astype(BF)
        normed[2 * b] = nb[:128]
        normed[2 * b + 1] = nb[128:]

    slot = xhi * 4 + z
    lead = core == 0
    sends = []
    for n in range(2):
        opposite = lead if n == 0 else jnp.logical_not(lead)
        for b in range(2):
            sends.append(pltpu.make_async_remote_copy(
                normed.at[2 * b + jnp.where(opposite, 1 - sw, sw)], xbuf.at[slot],
                a_send.at[2 * n + b], a_recv.at[slot],
                device_id=at(y, 1 - xlo, jnp.where(opposite, sopp, z), b, core),
                device_id_type=MESH))

    def relay(b):
        return pltpu.make_async_remote_copy(
            normed.at[2 * b + sw], rbuf.at[b], r_send.at[b], r_recv.at[b],
            device_id=at(y, xlo, sflip, xhi, core), device_id_type=MESH)

    def relayed(b):
        return pltpu.make_async_remote_copy(
            rbuf.at[b], xbuf.at[xhi * 4 + sflip], rf_send.at[b], a_recv.at[xhi * 4 + sflip],
            device_id=at(y, 1 - xlo, z, b, core), device_id_type=MESH)

    for c in sends[:2]:
        c.start()

    @pl.when(lead)
    def _():
        relay(0).start()
        relay(1).start()

    for c in sends[2:]:
        c.start()

    tsends = []
    for d in range(1, 8):
        to = (me + d) % 8
        for b in range(2):
            tsends.append(pltpu.make_async_remote_copy(
                perm.at[b, pl.ds(2 * to, 2)], tokch_ref.at[:, 2 * me + b],
                t_send.at[2 * d + b - 2], t_recv.at[2 * d + b - 2],
                device_id={"band": to, "loc": loc}, device_id_type=MESH))
    tlocal = [pltpu.make_async_copy(
        perm.at[b, pl.ds(2 * me, 2)], tokch_ref.at[:, 2 * me + b], t_local.at[b]) for b in range(2)]
    for c in tlocal:
        c.start()

    for c in wcopies:
        c.wait()

    def project(s, shared_q):
        x = xbuf[s]
        q = jnp.dot(x, wbuf[:, 0:256], preferred_element_type=F32) * QSCALE
        qbuf[s] = q[:, :128].astype(BF)
        if shared_q:
            qbuf[16 + s] = q[:, 128:].astype(BF)
        k = jnp.dot(x, wbuf[:, 256:512], preferred_element_type=F32)
        kbuf[0, s] = k[:, :128].astype(BF)
        kbuf[1, s] = k[:, 128:].astype(BF)
        v = jnp.dot(x, wbuf[:, 512:768], preferred_element_type=F32)
        vt = v.T.astype(BF)
        for n in range(4):
            vbuf[n, s, 0:64, :] = vt[64 * n:64 * n + 64]

    ones = jnp.ones((16, 128), BF)

    def fill(s, _):
        for n in range(4):
            vbuf[n, s, 64:80, :] = ones
        return 0

    lax.fori_loop(0, 16, fill, 0)

    def arrival(s):
        return pltpu.make_async_remote_copy(
            xbuf.at[s], xbuf.at[s], c_send.at[s], a_recv.at[s],
            device_id=at(y, xlo, z, xhi, 1 - core), device_id_type=MESH)

    def to_partner(s):
        return pltpu.make_async_remote_copy(
            xbuf.at[s], xbuf.at[8 + s], c_send.at[s], c_recv.at[s],
            device_id=at(y, xlo, z, xhi, 1 - core), device_id_type=MESH)

    def forward(s, n):
        return pltpu.make_async_remote_copy(
            xbuf.at[s], xbuf.at[s], f_send.at[n], a_recv.at[s],
            device_id=at(y, xlo, flip, xhi, core), device_id_type=MESH)

    def source(t, zero):
        r = t // 2
        early = jnp.where(zero == (r == 0), opp, z)
        return (t % 2) * 4 + jnp.where(r < 2, early, jnp.where(r == 2, flip, far))

    def arrive(t, _):
        @pl.when(t < 8)
        def _():
            s = source(t, lead)
            arrival(s).wait_recv()
            to_partner(s).start()

            @pl.when(s % 4 == opp)
            def _():
                forward(s, t % 2).start()

            @pl.when(jnp.logical_and(s % 4 == z, jnp.logical_not(lead)))
            def _():
                forward(s, 2 + t % 2).start()

            @pl.when(jnp.logical_and(t < 2, lead))
            def _():
                relay(t).wait_recv()
                relayed(t).start()

            @pl.when(t == TOK)
            def _():
                for c in tsends:
                    c.start()

            project(s, True)

        @pl.when(t >= 2)
        def _():
            s = source(t - 2, jnp.logical_not(lead))
            to_partner(s).wait_recv()
            project(8 + s, False)

        return 0

    lax.fori_loop(0, 10, arrive, 0)

    lane = lax.broadcasted_iota(jnp.int32, (256, 128), 1)

    def scores(u, h, sref, mref):
        kv = u // 8
        q = qbuf[pl.ds(2 * u, 2)].reshape(256, 128)
        q = jnp.where((lane < 64) == (h == 0), q, jnp.zeros_like(q))
        peak = None
        for c in range(8):
            keys = kbuf[kv, pl.ds(2 * c, 2)].reshape(256, 128)
            st = lax.dot_general(keys, q, NT, preferred_element_type=F32)
            sref[pl.ds(c * 256, 256), :] = st
            top = jnp.max(st.reshape(32, 8, 256), axis=0)
            peak = top if peak is None else jnp.maximum(peak, top)
        mref[...] = jnp.broadcast_to(jnp.max(peak, axis=0, keepdims=True), (8, 256))

    def mix(u, h, sref, mref):
        kv = u // 8
        peak = mref[0:1, :]
        acc = None
        for c in range(8):
            p = jnp.exp2(sref[pl.ds(c * 256, 256), :] - peak).astype(BF)
            for n in range(2):
                part = jnp.dot(vbuf[kv * 2 + h, 2 * c + n], p[128 * n:128 * n + 128],
                               preferred_element_type=F32)
                acc = part if acc is None else acc + part
        return acc[:64] / acc[64:65]

    band = 2 * (y * 2 + 1 - xlo) + xhi

    def send_out(i):
        s = i % 16
        src_core = (core + s // 8) % 2
        xs = (s % 8) // 4
        zs = s % 4
        pair = first + jnp.where(i < 16, core, 2)
        to_loc = zs * 4 + xs * 2 + src_core
        cols = pl.ds(pl.multiple_of(pair * 128, 128), 128)
        dst = sattn_ref.at[:, band, :, cols]

        def remote(jj):
            pltpu.make_async_remote_copy(
                obuf.at[pl.ds(8 * i + 2 * jj, 2)], dst, o_send, o_recv,
                device_id={"band": w * 4 + jj, "loc": to_loc}, device_id_type=MESH).start()

        own = jnp.logical_and(me // 4 == w, to_loc == loc)

        @pl.when(own)
        def _():
            for jj in range(4):
                @pl.when(w * 4 + jj == me)
                def _():
                    pltpu.make_async_copy(
                        obuf.at[pl.ds(8 * i + 2 * jj, 2)], dst, o_recv).start()

                @pl.when(w * 4 + jj != me)
                def _():
                    remote(jj)

        @pl.when(jnp.logical_not(own))
        def _():
            for jj in range(4):
                remote(jj)

    scores(0, 0, s0, m0)

    def unit(u, _):
        @pl.when(u > 0)
        def _():
            send_out(2 * u - 2)
            send_out(2 * u - 1)

        scores(u, 1, s1, m1)
        a = mix(u, 0, s0, m0)
        scores(jnp.minimum(u + 1, 11), 0, s0, m0)
        b = mix(u, 1, s1, m1)
        o = jnp.concatenate([a, b], axis=0).T.astype(BF)
        obuf[pl.ds(16 * u, 16)] = o.reshape(16, 16, 128)
        return 0

    lax.fori_loop(0, 12, unit, 0)
    send_out(22)
    send_out(23)

    for c in sends:
        c.wait_send()
    for n in range(2):
        forward(n * 4 + opp, n).wait_send()

    @pl.when(lead)
    def _():
        for b in range(2):
            relay(b).wait_send()
            relayed(b).wait_send()

    @pl.when(jnp.logical_not(lead))
    def _():
        for n in range(2):
            forward(n * 4 + z, 2 + n).wait_send()


    def core_done(s, _):
        to_partner(s).wait_send()
        return 0

    lax.fori_loop(0, 8, core_done, 0)
    for c in tsends:
        c.wait_send()
        c.wait_recv()
    for c in tlocal:
        c.wait()

    stays = me // 4 == w

    @pl.when(stays)
    def _():
        pltpu.make_async_copy(obuf.at[pl.ds(0, 188)], obuf.at[pl.ds(0, 188)], o_send).wait()

    @pl.when(jnp.logical_not(stays))
    def _():
        pltpu.make_async_copy(obuf, obuf, o_send).wait()

    pltpu.make_async_copy(sattn_ref, sattn_ref, o_recv).wait()

    embed = jnp.concatenate([table_ref[pl.ds(bi_ref[n], 1), :] for n in range(16)], axis=0)
    rowi = lax.broadcasted_iota(jnp.int32, (256, 256), 0)
    coli = lax.broadcasted_iota(jnp.int32, (256, 256), 1)
    same = (rowi % 16) == (coli % 16)

    def home(h, d):
        to = (me + d) % 8
        return pltpu.make_async_remote_copy(
            jbuf.at[h, pl.ds(2 * to, 2)], outp.at[:, 2 * me + h],
            j_send.at[8 * h + d], j_recv.at[8 * h + d],
            device_id={"band": to, "loc": loc}, device_id_type=MESH)

    def local(h):
        return pltpu.make_async_copy(
            jbuf.at[h, pl.ds(2 * me, 2)], outp.at[:, 2 * me + h], j_local.at[h])

    def half(h, _):
        start = (tokch_ref[h].astype(F32) + embed[:, None, :]).reshape(256, 768)
        mid = (start + jnp.dot(sattn_ref[h].reshape(256, 768), wo[...],
                               preferred_element_type=F32)).astype(BF)
        midf = mid.astype(F32)
        normed = norm_rows(midf).astype(BF)
        qc[...] = (jnp.dot(normed, wc[:, 0:768], preferred_element_type=F32) * QSCALE).astype(BF)
        kc[...] = jnp.dot(normed, wc[:, 768:1536], preferred_element_type=F32).astype(BF)
        vc[...] = jnp.dot(normed, wc[:, 1536:2304], preferred_element_type=F32).astype(BF)
        for pair in range(6):
            cols = pl.ds(pair * 128, 128)
            q = qc[:, cols]
            k = kc[:, cols]
            vx = jnp.concatenate([vc[:, cols], jnp.ones((256, 128), BF)], axis=1)
            res = []
            for n in range(2):
                qn = jnp.where((lane < 64) == (n == 0), q, jnp.zeros_like(q))
                s = lax.dot_general(qn, k, NT, preferred_element_type=F32)
                s = jnp.where(same, s, -1e30)
                p = jnp.exp2(s - jnp.max(s, axis=1, keepdims=True)).astype(BF)
                r = jnp.dot(p, vx, preferred_element_type=F32)
                res.append(r[:, :128] / r[:, 128:])
            cat[:, cols] = jnp.where(lane < 64, res[0], res[1]).astype(BF)
        after = midf + jnp.dot(cat[...], wco[...], preferred_element_type=F32)
        nrm[...] = norm_rows(after).astype(BF)
        aft[...] = after
        for g in range(2):
            rows_g = pl.ds(128 * g, 128)
            x = nrm[rows_g, :]
            for c in range(4):
                cols = pl.ds(c * 768, 768)
                up = jnp.dot(x, wu[:, cols], preferred_element_type=F32)
                hid[rows_g, cols] = jax.nn.gelu(up, approximate=True).astype(BF)
            joined = aft[rows_g, :] + jnp.dot(hid[rows_g, :], wd[...], preferred_element_type=F32)
            jbuf[h, pl.ds(8 * g, 8)] = joined.astype(BF).reshape(8, 16, 768)
            for d in range(1, 8):
                @pl.when(((me + d) % 8) // 4 == g)
                def _():
                    home(h, d).start()
        local(h).start()
        return 0

    for c in lcopies:
        c.wait()
    lax.fori_loop(0, 2, half, 0)
    for h in range(2):
        local(h).wait()
        for d in range(1, 8):
            home(h, d).wait_send()
            home(h, d).wait_recv()
    for b in range(2):
        out_ref[:, b, :] = lax.dot_general(
            choose[...], outp[b].reshape(256, 768), (((0,), (0,)), ((), ())),
            preferred_element_type=F32).astype(BF)


def layer(tokens, window_ids, band_index, table, spatial_qkv, weights):
    vmem = pl.BlockSpec(memory_space=pltpu.VMEM)
    hbm = pl.BlockSpec(memory_space=pl.ANY)
    dma = pltpu.SemaphoreType.DMA
    rows = pltpu.VMEM((2, 16, 16, 768), BF)
    return pl.pallas_call(
        layer_kernel,
        out_shape=jax.ShapeDtypeStruct((256, 2, 768), BF),
        in_specs=[vmem, vmem, pl.BlockSpec(memory_space=pltpu.SMEM), vmem] + [hbm] * 6,
        out_specs=vmem,
        scratch_shapes=[
            rows,
            pltpu.VMEM((4, 128, 768), BF),
            pltpu.VMEM((16, 128, 768), BF),
            pltpu.VMEM((768, 768), BF),
            pltpu.VMEM((24, 128, 128), BF),
            pltpu.VMEM((2, 16, 128, 128), BF),
            pltpu.VMEM((4, 16, 80, 128), BF),
            pltpu.VMEM((2048, 256), F32),
            pltpu.VMEM((2048, 256), F32),
            pltpu.VMEM((8, 256), F32),
            pltpu.VMEM((8, 256), F32),
            pltpu.VMEM((192, 16, 128), BF),
            pltpu.VMEM((256, 256), BF),
            pltpu.VMEM((2, 128, 768), BF),
        ] + [pltpu.VMEM(w.shape, BF) for w in weights] + [
            rows, rows, rows, rows,
            pltpu.VMEM((256, 768), BF),
            pltpu.VMEM((256, 768), BF),
            pltpu.VMEM((256, 768), F32),
            pltpu.VMEM((256, 768), BF),
            pltpu.VMEM((256, 768), BF),
            pltpu.VMEM((256, 768), BF),
            pltpu.VMEM((256, 3072), BF),
            dma((6,)), dma((4,)), dma((8,)), dma((4,)), dma((8,)), dma((8,)),
            dma((2,)), dma((2,)), dma((2,)),
            dma((14,)), dma((14,)), dma((2,)), dma, dma,
            dma((5,)), dma((16,)), dma((16,)), dma((2,)),
        ],
        compiler_params=pltpu.CompilerParams(
            has_side_effects=True, vmem_limit_bytes=60 << 20),
        name="layer",
    )(tokens, window_ids, band_index, table, spatial_qkv, *weights)


def body(
    tokens, band_index, band_table, window_ids, spatial_qkv, spatial_out,
    channel_qkv, channel_out, up_weight, down_weight,
):
    return layer(
        tokens, window_ids.reshape(32, 128), band_index, band_table, spatial_qkv,
        (spatial_out, channel_qkv, channel_out, up_weight, down_weight))


def solution(mesh):
    placed = (P("loc", "band", None), P(), P(), P(), P(), P(), P(), P(), P(), P())
    return jax.shard_map(
        body, mesh=mesh, in_specs=placed, out_specs=P("loc", "band", None), check_vma=False
    )
```

```python
import functools

import jax
import jax.numpy as jnp
from jax import lax
from jax.experimental import pallas as pl
from jax.experimental.pallas import tpu as pltpu
from jax.sharding import PartitionSpec as P

BF = jnp.bfloat16
F32 = jnp.float32
MESH = pl.DeviceIdType.MESH
NT = (((1,), (1,)), ((), ()))
TOK = 6
QSCALE = 0.125 * 1.4426950408889634


def norm_rows(values):
    centre = values - jnp.mean(values, axis=-1, keepdims=True)
    spread = jnp.mean(centre * centre, axis=-1, keepdims=True)
    return centre * lax.rsqrt(spread + 1e-05)


def place():
    band = lax.axis_index("band")
    loc = lax.axis_index("loc")
    return band // 2, band % 2, loc // 4, (loc // 2) % 2, loc % 2


def at(y, xlo, z, xhi, core):
    return {"band": y * 2 + xlo, "loc": z * 4 + xhi * 2 + core}


def layer_kernel(
    tok_ref, ids_ref, bi_ref, table_ref, w_hbm, wo_h, wc_h, wco_h, wu_h, wd_h,
    outp, choose_ref,
    perm, normed, xbuf, wbuf, qbuf, kbuf, vbuf, s0, s1, m0, m1, obuf,
    choose, rbuf, wo, wc, wco, wu, wd, sattn_ref, tokch_ref, jbuf, cat, nrm, aft, qc, kc, vc, hid,
    wsem, a_send, a_recv, f_send, c_send, c_recv, r_send, r_recv, rf_send, t_send, t_recv, t_local, o_send, o_recv,
    lsem, j_send, j_recv, j_local,
):
    y, xlo, z, xhi, core = place()
    me = lax.axis_index("band")
    loc = lax.axis_index("loc")

    def pairing(odd):
        turned = (z + 3 * odd) % 4
        beside = turned + 1 - 2 * (turned % 2)
        return turned, (beside + odd) % 4, (3 - turned + odd) % 4, (3 - beside + odd) % 4

    turned, flip, opp, far = pairing(xlo)
    sturned, sflip, sopp, _ = pairing(1 - xlo)
    w = turned // 2
    sw = sturned // 2

    first = 3 * (turned % 2)
    wcopies = []
    for t in range(3):
        for n, pair in enumerate((first + core, first + 2)):
            cols = pl.ds(pl.multiple_of(t * 768 + pair * 128, 128), 128)
            wcopies.append(pltpu.make_async_copy(
                w_hbm.at[:, cols], wbuf.at[:, pl.ds(t * 256 + n * 128, 128)], wsem.at[2 * t + n]))
    for c in wcopies:
        c.start()
    lcopies = [pltpu.make_async_copy(src, dst, lsem.at[n]) for n, (src, dst) in enumerate(
        ((wo_h, wo), (wc_h, wc), (wco_h, wco), (wu_h, wu), (wd_h, wd)))]
    for c in lcopies:
        c.start()

    ids = jnp.concatenate(
        [ids_ref[pl.ds(2 * loc, 1), :], ids_ref[pl.ds(2 * loc + 1, 1), :]], axis=1)
    down = lax.broadcasted_iota(jnp.int32, (256, 256), 0)
    across = lax.broadcasted_iota(jnp.int32, (256, 256), 1)
    ones_row = jnp.broadcast_to(ids.astype(F32), (8, 256)).astype(BF)
    earlier = jnp.where(down < across, 1.0, 0.0).astype(BF)
    before = jnp.dot(ones_row, earlier, preferred_element_type=F32)[0:1].astype(jnp.int32)
    count = lax.broadcasted_iota(jnp.int32, (1, 256), 1) - before
    target = jnp.where(ids == 1, 128 + before, count)
    select = jnp.where(down == target, 1.0, 0.0).astype(BF)
    choose[...] = select
    for b in range(2):
        part = jnp.dot(select, tok_ref[:, b, :], preferred_element_type=F32)
        perm[b] = part.astype(BF).reshape(16, 16, 768)
        row = table_ref[pl.ds(bi_ref[2 * me + b], 1), :]
        nb = norm_rows(part + row).astype(BF)
        normed[2 * b] = nb[:128]
        normed[2 * b + 1] = nb[128:]

    slot = xhi * 4 + z
    lead = core == 0
    sends = []
    for n in range(2):
        opposite = lead if n == 0 else jnp.logical_not(lead)
        for b in range(2):
            sends.append(pltpu.make_async_remote_copy(
                normed.at[2 * b + jnp.where(opposite, 1 - sw, sw)], xbuf.at[slot],
                a_send.at[2 * n + b], a_recv.at[slot],
                device_id=at(y, 1 - xlo, jnp.where(opposite, sopp, z), b, core),
                device_id_type=MESH))

    def relay(b):
        return pltpu.make_async_remote_copy(
            normed.at[2 * b + sw], rbuf.at[b], r_send.at[b], r_recv.at[b],
            device_id=at(y, xlo, sflip, xhi, core), device_id_type=MESH)

    def relayed(b):
        return pltpu.make_async_remote_copy(
            rbuf.at[b], xbuf.at[xhi * 4 + sflip], rf_send.at[b], a_recv.at[xhi * 4 + sflip],
            device_id=at(y, 1 - xlo, z, b, core), device_id_type=MESH)

    for c in sends[:2]:
        c.start()

    @pl.when(lead)
    def _():
        relay(0).start()
        relay(1).start()

    for c in sends[2:]:
        c.start()

    tsends = []
    for d in range(1, 8):
        to = (me + d) % 8
        for b in range(2):
            tsends.append(pltpu.make_async_remote_copy(
                perm.at[b, pl.ds(2 * to, 2)], tokch_ref.at[:, 2 * me + b],
                t_send.at[2 * d + b - 2], t_recv.at[2 * d + b - 2],
                device_id={"band": to, "loc": loc}, device_id_type=MESH))
    tlocal = [pltpu.make_async_copy(
        perm.at[b, pl.ds(2 * me, 2)], tokch_ref.at[:, 2 * me + b], t_local.at[b]) for b in range(2)]
    for c in tlocal:
        c.start()

    for c in wcopies:
        c.wait()

    def project(s, shared_q):
        x = xbuf[s]
        q = jnp.dot(x, wbuf[:, 0:256], preferred_element_type=F32) * QSCALE
        qbuf[s] = q[:, :128].astype(BF)
        if shared_q:
            qbuf[16 + s] = q[:, 128:].astype(BF)
        k = jnp.dot(x, wbuf[:, 256:512], preferred_element_type=F32)
        kbuf[0, s] = k[:, :128].astype(BF)
        kbuf[1, s] = k[:, 128:].astype(BF)
        v = jnp.dot(x, wbuf[:, 512:768], preferred_element_type=F32)
        vt = v.T.astype(BF)
        for n in range(4):
            vbuf[n, s, 0:64, :] = vt[64 * n:64 * n + 64]

    ones = jnp.ones((16, 128), BF)

    def fill(s, _):
        for n in range(4):
            vbuf[n, s, 64:80, :] = ones
        return 0

    lax.fori_loop(0, 16, fill, 0)

    def arrival(s):
        return pltpu.make_async_remote_copy(
            xbuf.at[s], xbuf.at[s], c_send.at[s], a_recv.at[s],
            device_id=at(y, xlo, z, xhi, 1 - core), device_id_type=MESH)

    def to_partner(s):
        return pltpu.make_async_remote_copy(
            xbuf.at[s], xbuf.at[8 + s], c_send.at[s], c_recv.at[s],
            device_id=at(y, xlo, z, xhi, 1 - core), device_id_type=MESH)

    def forward(s, n):
        return pltpu.make_async_remote_copy(
            xbuf.at[s], xbuf.at[s], f_send.at[n], a_recv.at[s],
            device_id=at(y, xlo, flip, xhi, core), device_id_type=MESH)

    def source(t, zero):
        r = t // 2
        early = jnp.where(zero == (r == 0), opp, z)
        return (t % 2) * 4 + jnp.where(r < 2, early, jnp.where(r == 2, flip, far))

    def arrive(t, _):
        @pl.when(t < 8)
        def _():
            s = source(t, lead)
            arrival(s).wait_recv()
            to_partner(s).start()

            @pl.when(s % 4 == opp)
            def _():
                forward(s, t % 2).start()

            @pl.when(jnp.logical_and(s % 4 == z, jnp.logical_not(lead)))
            def _():
                forward(s, 2 + t % 2).start()

            @pl.when(jnp.logical_and(t < 2, lead))
            def _():
                relay(t).wait_recv()
                relayed(t).start()

            @pl.when(t == TOK)
            def _():
                for c in tsends:
                    c.start()

            project(s, True)

        @pl.when(t >= 2)
        def _():
            s = source(t - 2, jnp.logical_not(lead))
            to_partner(s).wait_recv()
            project(8 + s, False)

        return 0

    lax.fori_loop(0, 10, arrive, 0)

    lane = lax.broadcasted_iota(jnp.int32, (256, 128), 1)

    def scores(u, h, sref, mref):
        kv = u // 8
        q = qbuf[pl.ds(2 * u, 2)].reshape(256, 128)
        q = jnp.where((lane < 64) == (h == 0), q, jnp.zeros_like(q))
        peak = None
        for c in range(8):
            keys = kbuf[kv, pl.ds(2 * c, 2)].reshape(256, 128)
            st = lax.dot_general(keys, q, NT, preferred_element_type=F32)
            sref[pl.ds(c * 256, 256), :] = st
            top = jnp.max(st.reshape(32, 8, 256), axis=0)
            peak = top if peak is None else jnp.maximum(peak, top)
        mref[...] = jnp.broadcast_to(jnp.max(peak, axis=0, keepdims=True), (8, 256))

    def mix(u, h, sref, mref):
        kv = u // 8
        peak = mref[0:1, :]
        acc = None
        for c in range(8):
            p = jnp.exp2(sref[pl.ds(c * 256, 256), :] - peak).astype(BF)
            for n in range(2):
                part = jnp.dot(vbuf[kv * 2 + h, 2 * c + n], p[128 * n:128 * n + 128],
                               preferred_element_type=F32)
                acc = part if acc is None else acc + part
        return acc[:64] / acc[64:65]

    band = 2 * (y * 2 + 1 - xlo) + xhi

    def send_out(i):
        s = i % 16
        src_core = (core + s // 8) % 2
        xs = (s % 8) // 4
        zs = s % 4
        pair = first + jnp.where(i < 16, core, 2)
        to_loc = zs * 4 + xs * 2 + src_core
        cols = pl.ds(pl.multiple_of(pair * 128, 128), 128)
        dst = sattn_ref.at[:, band, :, cols]

        def remote(jj):
            pltpu.make_async_remote_copy(
                obuf.at[pl.ds(8 * i + 2 * jj, 2)], dst, o_send, o_recv,
                device_id={"band": w * 4 + jj, "loc": to_loc}, device_id_type=MESH).start()

        own = jnp.logical_and(me // 4 == w, to_loc == loc)

        @pl.when(own)
        def _():
            for jj in range(4):
                @pl.when(w * 4 + jj == me)
                def _():
                    pltpu.make_async_copy(
                        obuf.at[pl.ds(8 * i + 2 * jj, 2)], dst, o_recv).start()

                @pl.when(w * 4 + jj != me)
                def _():
                    remote(jj)

        @pl.when(jnp.logical_not(own))
        def _():
            for jj in range(4):
                remote(jj)

    scores(0, 0, s0, m0)

    def unit(u, _):
        @pl.when(u > 0)
        def _():
            send_out(2 * u - 2)
            send_out(2 * u - 1)

        scores(u, 1, s1, m1)
        a = mix(u, 0, s0, m0)
        scores(jnp.minimum(u + 1, 11), 0, s0, m0)
        b = mix(u, 1, s1, m1)
        o = jnp.concatenate([a, b], axis=0).T.astype(BF)
        obuf[pl.ds(16 * u, 16)] = o.reshape(16, 16, 128)
        return 0

    lax.fori_loop(0, 12, unit, 0)
    send_out(22)
    send_out(23)

    for c in sends:
        c.wait_send()
    for n in range(2):
        forward(n * 4 + opp, n).wait_send()

    @pl.when(lead)
    def _():
        for b in range(2):
            relay(b).wait_send()
            relayed(b).wait_send()

    @pl.when(jnp.logical_not(lead))
    def _():
        for n in range(2):
            forward(n * 4 + z, 2 + n).wait_send()


    def core_done(s, _):
        to_partner(s).wait_send()
        return 0

    lax.fori_loop(0, 8, core_done, 0)
    for c in tsends:
        c.wait_send()
        c.wait_recv()
    for c in tlocal:
        c.wait()

    stays = me // 4 == w

    @pl.when(stays)
    def _():
        pltpu.make_async_copy(obuf.at[pl.ds(0, 188)], obuf.at[pl.ds(0, 188)], o_send).wait()

    @pl.when(jnp.logical_not(stays))
    def _():
        pltpu.make_async_copy(obuf, obuf, o_send).wait()

    pltpu.make_async_copy(sattn_ref, sattn_ref, o_recv).wait()

    embed = jnp.concatenate([table_ref[pl.ds(bi_ref[n], 1), :] for n in range(16)], axis=0)
    rowi = lax.broadcasted_iota(jnp.int32, (256, 256), 0)
    coli = lax.broadcasted_iota(jnp.int32, (256, 256), 1)
    same = (rowi % 16) == (coli % 16)

    def home(h, d):
        to = (me + d) % 8
        return pltpu.make_async_remote_copy(
            jbuf.at[h, pl.ds(2 * to, 2)], outp.at[:, 2 * me + h],
            j_send.at[8 * h + d], j_recv.at[8 * h + d],
            device_id={"band": to, "loc": loc}, device_id_type=MESH)

    def local(h):
        return pltpu.make_async_copy(
            jbuf.at[h, pl.ds(2 * me, 2)], outp.at[:, 2 * me + h], j_local.at[h])

    def half(h, _):
        start = (tokch_ref[h].astype(F32) + embed[:, None, :]).reshape(256, 768)
        mid = (start + jnp.dot(sattn_ref[h].reshape(256, 768), wo[...],
                               preferred_element_type=F32)).astype(BF)
        midf = mid.astype(F32)
        normed = norm_rows(midf).astype(BF)
        qc[...] = (jnp.dot(normed, wc[:, 0:768], preferred_element_type=F32) * QSCALE).astype(BF)
        kc[...] = jnp.dot(normed, wc[:, 768:1536], preferred_element_type=F32).astype(BF)
        vc[...] = jnp.dot(normed, wc[:, 1536:2304], preferred_element_type=F32).astype(BF)
        for pair in range(6):
            cols = pl.ds(pair * 128, 128)
            q = qc[:, cols]
            k = kc[:, cols]
            vx = jnp.concatenate([vc[:, cols], jnp.ones((256, 128), BF)], axis=1)
            res = []
            for n in range(2):
                qn = jnp.where((lane < 64) == (n == 0), q, jnp.zeros_like(q))
                s = lax.dot_general(qn, k, NT, preferred_element_type=F32)
                s = jnp.where(same, s, -1e30)
                p = jnp.exp2(s - jnp.max(s, axis=1, keepdims=True)).astype(BF)
                r = jnp.dot(p, vx, preferred_element_type=F32)
                res.append(r[:, :128] / r[:, 128:])
            cat[:, cols] = jnp.where(lane < 64, res[0], res[1]).astype(BF)
        after = midf + jnp.dot(cat[...], wco[...], preferred_element_type=F32)
        nrm[...] = norm_rows(after).astype(BF)
        aft[...] = after
        for g in range(2):
            rows_g = pl.ds(128 * g, 128)
            x = nrm[rows_g, :]
            for c in range(4):
                cols = pl.ds(c * 768, 768)
                up = jnp.dot(x, wu[:, cols], preferred_element_type=F32)
                hid[rows_g, cols] = jax.nn.gelu(up, approximate=True).astype(BF)
            joined = aft[rows_g, :] + jnp.dot(hid[rows_g, :], wd[...], preferred_element_type=F32)
            jbuf[h, pl.ds(8 * g, 8)] = joined.astype(BF).reshape(8, 16, 768)
            for d in range(1, 8):
                @pl.when(((me + d) % 8) // 4 == g)
                def _():
                    home(h, d).start()
        local(h).start()
        return 0

    for c in lcopies:
        c.wait()
    lax.fori_loop(0, 2, half, 0)
    for h in range(2):
        local(h).wait()
        for d in range(1, 8):
            home(h, d).wait_send()
            home(h, d).wait_recv()
    choose_ref[...] = choose[...]


def restore_kernel(rows_ref, choose_ref, out_ref):
    for b in range(2):
        out_ref[:, b, :] = lax.dot_general(
            choose_ref[...], rows_ref[b].reshape(256, 256), (((0,), (0,)), ((), ())),
            preferred_element_type=F32).astype(BF)


def layer(tokens, window_ids, band_index, table, spatial_qkv, weights):
    vmem = pl.BlockSpec(memory_space=pltpu.VMEM)
    hbm = pl.BlockSpec(memory_space=pl.ANY)
    dma = pltpu.SemaphoreType.DMA
    rows = pltpu.VMEM((2, 16, 16, 768), BF)
    ordered, choose = pl.pallas_call(
        layer_kernel,
        out_shape=[jax.ShapeDtypeStruct((2, 16, 16, 768), BF), jax.ShapeDtypeStruct((256, 256), BF)],
        in_specs=[vmem, vmem, pl.BlockSpec(memory_space=pltpu.SMEM), vmem] + [hbm] * 6,
        out_specs=[hbm, vmem],
        scratch_shapes=[
            rows,
            pltpu.VMEM((4, 128, 768), BF),
            pltpu.VMEM((16, 128, 768), BF),
            pltpu.VMEM((768, 768), BF),
            pltpu.VMEM((24, 128, 128), BF),
            pltpu.VMEM((2, 16, 128, 128), BF),
            pltpu.VMEM((4, 16, 80, 128), BF),
            pltpu.VMEM((2048, 256), F32),
            pltpu.VMEM((2048, 256), F32),
            pltpu.VMEM((8, 256), F32),
            pltpu.VMEM((8, 256), F32),
            pltpu.VMEM((192, 16, 128), BF),
            pltpu.VMEM((256, 256), BF),
            pltpu.VMEM((2, 128, 768), BF),
        ] + [pltpu.VMEM(w.shape, BF) for w in weights] + [
            rows, rows, rows,
            pltpu.VMEM((256, 768), BF),
            pltpu.VMEM((256, 768), BF),
            pltpu.VMEM((256, 768), F32),
            pltpu.VMEM((256, 768), BF),
            pltpu.VMEM((256, 768), BF),
            pltpu.VMEM((256, 768), BF),
            pltpu.VMEM((256, 3072), BF),
            dma((6,)), dma((4,)), dma((8,)), dma((4,)), dma((8,)), dma((8,)),
            dma((2,)), dma((2,)), dma((2,)),
            dma((14,)), dma((14,)), dma((2,)), dma, dma,
            dma((5,)), dma((16,)), dma((16,)), dma((2,)),
        ],
        compiler_params=pltpu.CompilerParams(
            has_side_effects=True, vmem_limit_bytes=60 << 20),
        name="layer",
    )(tokens, window_ids, band_index, table, spatial_qkv, *weights)
    return pl.pallas_call(
        restore_kernel,
        out_shape=jax.ShapeDtypeStruct((256, 2, 768), BF),
        grid=(3,),
        in_specs=[
            pl.BlockSpec((2, 16, 16, 256), lambda i: (0, 0, 0, i)),
            pl.BlockSpec((256, 256), lambda i: (0, 0)),
        ],
        out_specs=pl.BlockSpec((256, 2, 256), lambda i: (0, 0, i)),
        name="restore",
    )(ordered, choose)


def body(
    tokens, band_index, band_table, window_ids, spatial_qkv, spatial_out,
    channel_qkv, channel_out, up_weight, down_weight,
):
    return layer(
        tokens, window_ids.reshape(32, 128), band_index, band_table, spatial_qkv,
        (spatial_out, channel_qkv, channel_out, up_weight, down_weight))


def solution(mesh):
    placed = (P("loc", "band", None), P(), P(), P(), P(), P(), P(), P(), P(), P())
    return jax.shard_map(
        body, mesh=mesh, in_specs=placed, out_specs=P("loc", "band", None), check_vma=False
    )
```

```python
import functools

import jax
import jax.numpy as jnp
from jax import lax
from jax.experimental import pallas as pl
from jax.experimental.pallas import tpu as pltpu
from jax.sharding import PartitionSpec as P

BF = jnp.bfloat16
F32 = jnp.float32
MESH = pl.DeviceIdType.MESH
NT = (((1,), (1,)), ((), ()))
TOK = 6
QSCALE = 0.125 * 1.4426950408889634


def norm_rows(values):
    centre = values - jnp.mean(values, axis=-1, keepdims=True)
    spread = jnp.mean(centre * centre, axis=-1, keepdims=True)
    return centre * lax.rsqrt(spread + 1e-05)


def place():
    band = lax.axis_index("band")
    loc = lax.axis_index("loc")
    return band // 2, band % 2, loc // 4, (loc // 2) % 2, loc % 2


def at(y, xlo, z, xhi, core):
    return {"band": y * 2 + xlo, "loc": z * 4 + xhi * 2 + core}


def layer_kernel(
    tok_ref, ids_ref, bi_ref, table_ref, w_hbm, wo_h, wc_h, wco_h, wu_h, wd_h,
    outp, choose_ref,
    perm, normed, xbuf, wbuf, qbuf, kbuf, vbuf, s0, s1, m0, m1, obuf,
    choose, rbuf, wo, wc, wco, wu, wd, sattn_ref, tokch_ref, jbuf, cat, nrm, aft, qc, kc, vc, hid,
    wsem, a_send, a_recv, f_send, c_send, c_recv, r_send, r_recv, rf_send, t_send, t_recv, t_local, o_send, o_recv,
    lsem, j_send, j_recv, j_local,
):
    y, xlo, z, xhi, core = place()
    me = lax.axis_index("band")
    loc = lax.axis_index("loc")

    def pairing(odd):
        turned = (z + 3 * odd) % 4
        beside = turned + 1 - 2 * (turned % 2)
        return turned, (beside + odd) % 4, (3 - turned + odd) % 4, (3 - beside + odd) % 4

    turned, flip, opp, far = pairing(xlo)
    sturned, sflip, sopp, _ = pairing(1 - xlo)
    w = turned // 2
    sw = sturned // 2

    first = 3 * (turned % 2)
    wcopies = []
    for t in range(3):
        for n, pair in enumerate((first + core, first + 2)):
            cols = pl.ds(pl.multiple_of(t * 768 + pair * 128, 128), 128)
            wcopies.append(pltpu.make_async_copy(
                w_hbm.at[:, cols], wbuf.at[:, pl.ds(t * 256 + n * 128, 128)], wsem.at[2 * t + n]))
    for c in wcopies:
        c.start()
    lcopies = [pltpu.make_async_copy(src, dst, lsem.at[n]) for n, (src, dst) in enumerate(
        ((wo_h, wo), (wc_h, wc), (wco_h, wco), (wu_h, wu), (wd_h, wd)))]
    for c in lcopies:
        c.start()

    ids = jnp.concatenate(
        [ids_ref[pl.ds(2 * loc, 1), :], ids_ref[pl.ds(2 * loc + 1, 1), :]], axis=1)
    down = lax.broadcasted_iota(jnp.int32, (256, 256), 0)
    across = lax.broadcasted_iota(jnp.int32, (256, 256), 1)
    ones_row = jnp.broadcast_to(ids.astype(F32), (8, 256)).astype(BF)
    earlier = jnp.where(down < across, 1.0, 0.0).astype(BF)
    before = jnp.dot(ones_row, earlier, preferred_element_type=F32)[0:1].astype(jnp.int32)
    count = lax.broadcasted_iota(jnp.int32, (1, 256), 1) - before
    target = jnp.where(ids == 1, 128 + before, count)
    select = jnp.where(down == target, 1.0, 0.0).astype(BF)
    choose[...] = select
    for b in range(2):
        part = jnp.dot(select, tok_ref[:, b, :], preferred_element_type=F32)
        perm[b] = part.astype(BF).reshape(16, 16, 768)
        row = table_ref[pl.ds(bi_ref[2 * me + b], 1), :]
        nb = norm_rows(part + row).astype(BF)
        normed[2 * b] = nb[:128]
        normed[2 * b + 1] = nb[128:]

    slot = xhi * 4 + z
    lead = core == 0
    sends = []
    for n in range(2):
        opposite = lead if n == 0 else jnp.logical_not(lead)
        for b in range(2):
            sends.append(pltpu.make_async_remote_copy(
                normed.at[2 * b + jnp.where(opposite, 1 - sw, sw)], xbuf.at[slot],
                a_send.at[2 * n + b], a_recv.at[slot],
                device_id=at(y, 1 - xlo, jnp.where(opposite, sopp, z), b, core),
                device_id_type=MESH))

    def relay(b):
        return pltpu.make_async_remote_copy(
            normed.at[2 * b + sw], rbuf.at[b], r_send.at[b], r_recv.at[b],
            device_id=at(y, xlo, sflip, xhi, core), device_id_type=MESH)

    def relayed(b):
        return pltpu.make_async_remote_copy(
            rbuf.at[b], xbuf.at[xhi * 4 + sflip], rf_send.at[b], a_recv.at[xhi * 4 + sflip],
            device_id=at(y, 1 - xlo, z, b, core), device_id_type=MESH)

    for c in sends[:2]:
        c.start()

    @pl.when(lead)
    def _():
        relay(0).start()
        relay(1).start()

    for c in sends[2:]:
        c.start()

    tsends = []
    for d in range(1, 8):
        to = (me + d) % 8
        for b in range(2):
            tsends.append(pltpu.make_async_remote_copy(
                perm.at[b, pl.ds(2 * to, 2)], tokch_ref.at[:, 2 * me + b],
                t_send.at[2 * d + b - 2], t_recv.at[2 * d + b - 2],
                device_id={"band": to, "loc": loc}, device_id_type=MESH))
    tlocal = [pltpu.make_async_copy(
        perm.at[b, pl.ds(2 * me, 2)], tokch_ref.at[:, 2 * me + b], t_local.at[b]) for b in range(2)]
    for c in tlocal:
        c.start()

    for c in wcopies:
        c.wait()

    def project(s, shared_q):
        x = xbuf[s]
        q = jnp.dot(x, wbuf[:, 0:256], preferred_element_type=F32) * QSCALE
        qbuf[s] = q[:, :128].astype(BF)
        if shared_q:
            qbuf[16 + s] = q[:, 128:].astype(BF)
        k = jnp.dot(x, wbuf[:, 256:512], preferred_element_type=F32)
        kbuf[0, s] = k[:, :128].astype(BF)
        kbuf[1, s] = k[:, 128:].astype(BF)
        v = jnp.dot(x, wbuf[:, 512:768], preferred_element_type=F32)
        vt = v.T.astype(BF)
        for n in range(4):
            vbuf[n, s, 0:64, :] = vt[64 * n:64 * n + 64]

    ones = jnp.ones((16, 128), BF)

    def fill(s, _):
        for n in range(4):
            vbuf[n, s, 64:80, :] = ones
        return 0

    lax.fori_loop(0, 16, fill, 0)

    def arrival(s):
        return pltpu.make_async_remote_copy(
            xbuf.at[s], xbuf.at[s], c_send.at[s], a_recv.at[s],
            device_id=at(y, xlo, z, xhi, 1 - core), device_id_type=MESH)

    def to_partner(s):
        return pltpu.make_async_remote_copy(
            xbuf.at[s], xbuf.at[8 + s], c_send.at[s], c_recv.at[s],
            device_id=at(y, xlo, z, xhi, 1 - core), device_id_type=MESH)

    def forward(s, n):
        return pltpu.make_async_remote_copy(
            xbuf.at[s], xbuf.at[s], f_send.at[n], a_recv.at[s],
            device_id=at(y, xlo, flip, xhi, core), device_id_type=MESH)

    def source(t, zero):
        r = t // 2
        early = jnp.where(zero == (r == 0), opp, z)
        return (t % 2) * 4 + jnp.where(r < 2, early, jnp.where(r == 2, flip, far))

    def arrive(t, _):
        @pl.when(t < 8)
        def _():
            s = source(t, lead)
            arrival(s).wait_recv()
            to_partner(s).start()

            @pl.when(s % 4 == opp)
            def _():
                forward(s, t % 2).start()

            @pl.when(jnp.logical_and(s % 4 == z, jnp.logical_not(lead)))
            def _():
                forward(s, 2 + t % 2).start()

            @pl.when(jnp.logical_and(t < 2, lead))
            def _():
                relay(t).wait_recv()
                relayed(t).start()

            @pl.when(t == TOK)
            def _():
                for c in tsends:
                    c.start()

            project(s, True)

        @pl.when(t >= 2)
        def _():
            s = source(t - 2, jnp.logical_not(lead))
            to_partner(s).wait_recv()
            project(8 + s, False)

        return 0

    lax.fori_loop(0, 10, arrive, 0)

    lane = lax.broadcasted_iota(jnp.int32, (256, 128), 1)

    def scores(u, h, sref, mref):
        kv = u // 8
        q = qbuf[pl.ds(2 * u, 2)].reshape(256, 128)
        q = jnp.where((lane < 64) == (h == 0), q, jnp.zeros_like(q))
        peak = None
        for c in range(8):
            keys = kbuf[kv, pl.ds(2 * c, 2)].reshape(256, 128)
            st = lax.dot_general(keys, q, NT, preferred_element_type=F32)
            sref[pl.ds(c * 256, 256), :] = st
            top = jnp.max(st.reshape(32, 8, 256), axis=0)
            peak = top if peak is None else jnp.maximum(peak, top)
        mref[...] = jnp.broadcast_to(jnp.max(peak, axis=0, keepdims=True), (8, 256))

    def mix(u, h, sref, mref):
        kv = u // 8
        peak = mref[0:1, :]
        acc = None
        for c in range(8):
            p = jnp.exp2(sref[pl.ds(c * 256, 256), :] - peak).astype(BF)
            for n in range(2):
                part = jnp.dot(vbuf[kv * 2 + h, 2 * c + n], p[128 * n:128 * n + 128],
                               preferred_element_type=F32)
                acc = part if acc is None else acc + part
        return acc[:64] / acc[64:65]

    band = 2 * (y * 2 + 1 - xlo) + xhi

    def send_out(i):
        s = i % 16
        src_core = (core + s // 8) % 2
        xs = (s % 8) // 4
        zs = s % 4
        pair = first + jnp.where(i < 16, core, 2)
        to_loc = zs * 4 + xs * 2 + src_core
        cols = pl.ds(pl.multiple_of(pair * 128, 128), 128)
        dst = sattn_ref.at[:, band, :, cols]

        def remote(jj):
            pltpu.make_async_remote_copy(
                obuf.at[pl.ds(8 * i + 2 * jj, 2)], dst, o_send, o_recv,
                device_id={"band": w * 4 + jj, "loc": to_loc}, device_id_type=MESH).start()

        own = jnp.logical_and(me // 4 == w, to_loc == loc)

        @pl.when(own)
        def _():
            for jj in range(4):
                @pl.when(w * 4 + jj == me)
                def _():
                    pltpu.make_async_copy(
                        obuf.at[pl.ds(8 * i + 2 * jj, 2)], dst, o_recv).start()

                @pl.when(w * 4 + jj != me)
                def _():
                    remote(jj)

        @pl.when(jnp.logical_not(own))
        def _():
            for jj in range(4):
                remote(jj)

    scores(0, 0, s0, m0)

    def unit(u, _):
        @pl.when(u > 0)
        def _():
            send_out(2 * u - 2)
            send_out(2 * u - 1)

        scores(u, 1, s1, m1)
        a = mix(u, 0, s0, m0)
        scores(jnp.minimum(u + 1, 11), 0, s0, m0)
        b = mix(u, 1, s1, m1)
        o = jnp.concatenate([a, b], axis=0).T.astype(BF)
        obuf[pl.ds(16 * u, 16)] = o.reshape(16, 16, 128)
        return 0

    lax.fori_loop(0, 12, unit, 0)
    send_out(22)
    send_out(23)

    for c in sends:
        c.wait_send()
    for n in range(2):
        forward(n * 4 + opp, n).wait_send()

    @pl.when(lead)
    def _():
        for b in range(2):
            relay(b).wait_send()
            relayed(b).wait_send()

    @pl.when(jnp.logical_not(lead))
    def _():
        for n in range(2):
            forward(n * 4 + z, 2 + n).wait_send()


    def core_done(s, _):
        to_partner(s).wait_send()
        return 0

    lax.fori_loop(0, 8, core_done, 0)
    for c in tsends:
        c.wait_send()
        c.wait_recv()
    for c in tlocal:
        c.wait()

    stays = me // 4 == w

    @pl.when(stays)
    def _():
        pltpu.make_async_copy(obuf.at[pl.ds(0, 188)], obuf.at[pl.ds(0, 188)], o_send).wait()

    @pl.when(jnp.logical_not(stays))
    def _():
        pltpu.make_async_copy(obuf, obuf, o_send).wait()

    pltpu.make_async_copy(sattn_ref, sattn_ref, o_recv).wait()

    embed = jnp.concatenate([table_ref[pl.ds(bi_ref[n], 1), :] for n in range(16)], axis=0)
    rowi = lax.broadcasted_iota(jnp.int32, (256, 256), 0)
    coli = lax.broadcasted_iota(jnp.int32, (256, 256), 1)
    same = (rowi % 16) == (coli % 16)

    def home(h, d):
        to = (me + d) % 8
        return pltpu.make_async_remote_copy(
            jbuf.at[h, pl.ds(2 * to, 2)], outp.at[:, 2 * me + h],
            j_send.at[8 * h + d], j_recv.at[8 * h + d],
            device_id={"band": to, "loc": loc}, device_id_type=MESH)

    def local(h):
        return pltpu.make_async_copy(
            jbuf.at[h, pl.ds(2 * me, 2)], outp.at[:, 2 * me + h], j_local.at[h])

    def half(h, _):
        start = (tokch_ref[h].astype(F32) + embed[:, None, :]).reshape(256, 768)
        mid = (start + jnp.dot(sattn_ref[h].reshape(256, 768), wo[...],
                               preferred_element_type=F32)).astype(BF)
        midf = mid.astype(F32)
        normed = norm_rows(midf).astype(BF)
        qc[...] = (jnp.dot(normed, wc[:, 0:768], preferred_element_type=F32) * QSCALE).astype(BF)
        kc[...] = jnp.dot(normed, wc[:, 768:1536], preferred_element_type=F32).astype(BF)
        vc[...] = jnp.dot(normed, wc[:, 1536:2304], preferred_element_type=F32).astype(BF)
        for pair in range(6):
            cols = pl.ds(pair * 128, 128)
            q = qc[:, cols]
            k = kc[:, cols]
            vx = jnp.concatenate([vc[:, cols], jnp.ones((256, 128), BF)], axis=1)
            res = []
            for n in range(2):
                qn = jnp.where((lane < 64) == (n == 0), q, jnp.zeros_like(q))
                s = lax.dot_general(qn, k, NT, preferred_element_type=F32)
                s = jnp.where(same, s, -1e30)
                p = jnp.exp2(s - jnp.max(s, axis=1, keepdims=True)).astype(BF)
                r = jnp.dot(p, vx, preferred_element_type=F32)
                res.append(r[:, :128] / r[:, 128:])
            cat[:, cols] = jnp.where(lane < 64, res[0], res[1]).astype(BF)
        after = midf + jnp.dot(cat[...], wco[...], preferred_element_type=F32)
        nrm[...] = norm_rows(after).astype(BF)
        aft[...] = after
        for g in range(2):
            rows_g = pl.ds(128 * g, 128)
            x = nrm[rows_g, :]
            for c in range(4):
                cols = pl.ds(c * 768, 768)
                up = jnp.dot(x, wu[:, cols], preferred_element_type=F32)
                hid[rows_g, cols] = jax.nn.gelu(up, approximate=True).astype(BF)
            joined = aft[rows_g, :] + jnp.dot(hid[rows_g, :], wd[...], preferred_element_type=F32)
            jbuf[h, pl.ds(8 * g, 8)] = joined.astype(BF).reshape(8, 16, 768)
            for d in range(1, 8):
                @pl.when(((me + d) % 8) // 4 == g)
                def _():
                    home(h, d).start()
        local(h).start()
        return 0

    for c in lcopies:
        c.wait()
    lax.fori_loop(0, 2, half, 0)
    for h in range(2):
        local(h).wait()
        for d in range(1, 8):
            home(h, d).wait_send()
            home(h, d).wait_recv()
    choose_ref[...] = choose[...]


def restore_kernel(rows_ref, choose_ref, out_ref):
    for b in range(2):
        out_ref[:, b, :] = lax.dot_general(
            choose_ref[...], rows_ref[b].reshape(256, 768), (((0,), (0,)), ((), ())),
            preferred_element_type=F32).astype(BF)


def layer(tokens, window_ids, band_index, table, spatial_qkv, weights):
    vmem = pl.BlockSpec(memory_space=pltpu.VMEM)
    hbm = pl.BlockSpec(memory_space=pl.ANY)
    dma = pltpu.SemaphoreType.DMA
    rows = pltpu.VMEM((2, 16, 16, 768), BF)
    ordered, choose = pl.pallas_call(
        layer_kernel,
        out_shape=[jax.ShapeDtypeStruct((2, 16, 16, 768), BF), jax.ShapeDtypeStruct((256, 256), BF)],
        in_specs=[vmem, vmem, pl.BlockSpec(memory_space=pltpu.SMEM), vmem] + [hbm] * 6,
        out_specs=[hbm, vmem],
        scratch_shapes=[
            rows,
            pltpu.VMEM((4, 128, 768), BF),
            pltpu.VMEM((16, 128, 768), BF),
            pltpu.VMEM((768, 768), BF),
            pltpu.VMEM((24, 128, 128), BF),
            pltpu.VMEM((2, 16, 128, 128), BF),
            pltpu.VMEM((4, 16, 80, 128), BF),
            pltpu.VMEM((2048, 256), F32),
            pltpu.VMEM((2048, 256), F32),
            pltpu.VMEM((8, 256), F32),
            pltpu.VMEM((8, 256), F32),
            pltpu.VMEM((192, 16, 128), BF),
            pltpu.VMEM((256, 256), BF),
            pltpu.VMEM((2, 128, 768), BF),
        ] + [pltpu.VMEM(w.shape, BF) for w in weights] + [
            rows, rows, rows,
            pltpu.VMEM((256, 768), BF),
            pltpu.VMEM((256, 768), BF),
            pltpu.VMEM((256, 768), F32),
            pltpu.VMEM((256, 768), BF),
            pltpu.VMEM((256, 768), BF),
            pltpu.VMEM((256, 768), BF),
            pltpu.VMEM((256, 3072), BF),
            dma((6,)), dma((4,)), dma((8,)), dma((4,)), dma((8,)), dma((8,)),
            dma((2,)), dma((2,)), dma((2,)),
            dma((14,)), dma((14,)), dma((2,)), dma, dma,
            dma((5,)), dma((16,)), dma((16,)), dma((2,)),
        ],
        compiler_params=pltpu.CompilerParams(
            has_side_effects=True, vmem_limit_bytes=60 << 20),
        name="layer",
    )(tokens, window_ids, band_index, table, spatial_qkv, *weights)
    return pl.pallas_call(
        restore_kernel,
        out_shape=jax.ShapeDtypeStruct((256, 2, 768), BF),
        in_specs=[vmem, vmem],
        out_specs=vmem,
        name="restore",
    )(ordered, choose)


def body(
    tokens, band_index, band_table, window_ids, spatial_qkv, spatial_out,
    channel_qkv, channel_out, up_weight, down_weight,
):
    return layer(
        tokens, window_ids.reshape(32, 128), band_index, band_table, spatial_qkv,
        (spatial_out, channel_qkv, channel_out, up_weight, down_weight))


def solution(mesh):
    placed = (P("loc", "band", None), P(), P(), P(), P(), P(), P(), P(), P(), P())
    return jax.shard_map(
        body, mesh=mesh, in_specs=placed, out_specs=P("loc", "band", None), check_vma=False
    )
```
